32 devices in a mesh: tract: 2 (over y), sky: 4 (over x, core), band: 4 (over z).
Axes of the slice: x: 2, y: 2, z: 4, core: 2. Of those that a mesh axis runs over, the one named last changes fastest.
Arguments:
- patches: float32 [8, 32, 256, 256], P(('tract', 'band'), 'sky'), parts along dimension 0, may hold values from -6 to 6
- valid_rows: int32 [8, 32], P(('tract', 'band'), 'sky'), parts along dimension 0, may hold values from 64 to 256
- slot_owner: int32 [8, 32, 1], P(('tract', 'band'), 'sky'), parts along dimension 0, may hold values from 0 to 3; in each aligned block of 8 rows (0 to 7, 8 to 15, ..., all dimensions but the last counted through in order) at most 4 rows name the same one
- slot_local: int32 [8, 32], P(('tract', 'band'), 'sky'), parts along dimension 0, may hold values from 0 to 7
- slot_visit: int32 [8, 32], P(('tract', 'band'), 'sky'), parts along dimension 0, may hold values from 0 to 11
- basis_coef: float32 [8, 12, 21], P(('tract', 'band')), parts along dimension 0, may hold values from -1.25 to 1.25
- inv_var: float32 [8, 12], P(('tract', 'band')), parts along dimension 0, may hold values from 0.1 to 1
- kernel_x: bfloat16 [21, 41], replicated, may hold values from -1 to 1
- kernel_y: bfloat16 [21, 41], replicated, may hold values from -1 to 1
Outputs:
- band_coadd: float32 [8, 32, 256, 256], P(('tract', 'band'), 'sky'), parts along dimension 0
- detection: float32 [64, 256, 256], P(('tract', 'sky'), 'band'), parts along dimension 0
The draws below stay inside these ranges and needn't reach their ends.
There are 2 independent parts, one for each index of `tract`. The reference program is written for one: setup_inputs(seed, part) draws one part's arguments, and reference() takes and returns one part's arrays. A program takes and returns all parts, laid end to end along the dimension named above; an argument that names none is the same for every part. Nothing has to cross between parts.
Inputs may be any that keep to these rules, and one draw needn't show every extreme that they name: `slot_owner`: among the pieces of one device no owner appears more than 4 times; some device gives exactly 4 pieces to one owner.
All inputs are finite; a program needn't handle non-finite values.
Results may differ from the reference program's by a relative error of at most 0.015.
Values may be sent and summed in bfloat16 or wider, within the bound.
A program may use at most 128 MiB of HBM per device.

```python
import math
import jax
import jax.numpy as jnp
import numpy as np
from jax import lax

P_SIZE = 256
KS = 41
NB = 21
VIS = 12
SLOTS_DEV = 8
PATCH_DEV = 8
CAP = 4
SLOTS = 32
PATCHES = 32
BANDS = 4
N_SKY = 4


def with_ends(values, rng, smallest, largest):
    place = [jax.random.randint(jax.random.fold_in(rng, axis), (), 0, length) for axis, length in enumerate(values.shape)]
    main_axis = values.shape.index(max(values.shape))
    next_to = place[:main_axis] + [(place[main_axis] + 1) % values.shape[main_axis]] + place[main_axis + 1:]
    return values.at[tuple(place)].set(smallest).at[tuple(next_to)].set(largest)


def block_scale(stream_key, extent, shards, least, high):
    factor_of = 1.0
    for axis_at, blocks in shards:
        heights = jax.random.uniform(jax.random.fold_in(jax.random.fold_in(stream_key, 6), axis_at), (blocks,), jnp.float32, least / len(shards), high / len(shards))
        factor_of = factor_of * jnp.repeat(jnp.exp(heights), extent[axis_at] // blocks).reshape((-1,) + (1,) * (len(extent) - 1 - axis_at))
    return factor_of


def shared_out(stream_key, own, number, rows, count, top, limit, lean):
    order = jax.random.permutation(stream_key, count)
    heavy_load, common = load_shares(count, rows * top, limit, lean, True), load_shares(count, rows * top, limit, lean, False)
    places = jnp.arange(count)

    def named(sizes, offset_by):
        used = int((sizes > 0).sum())
        fixed = max(1, used // 4)
        passed = fixed + (places - fixed + offset_by * (used - fixed)) % max(1, count - fixed)
        return jnp.zeros((count,), jnp.int32).at[order[jnp.where(places < fixed, places, passed)]].set(jnp.asarray(sizes, jnp.int32))

    sizes = jnp.where(number % 4 == 0, named(heavy_load, number // 4), named(common, number - number // 4 - 1))
    mixed = jax.random.permutation(jax.random.fold_in(own, 3), count)
    donor, receiver = mixed[0:count // 2 * 2:2], mixed[1:count // 2 * 2:2]
    room = jnp.minimum(sizes[donor] - 1, limit - sizes[receiver]) // 2
    room = jnp.where((donor == order[0]) | (receiver == order[0]) | (sizes[receiver] == 0), 0, jnp.maximum(room, 0))
    passed = jax.random.randint(jax.random.fold_in(own, 4), (count // 2,), 0, 1 << 20) % (room + 1)
    sizes = sizes.at[donor].add(-passed).at[receiver].add(passed)
    items = jnp.searchsorted(jnp.cumsum(sizes), jnp.arange(rows * top), side="right").astype(jnp.int32)
    table = items.reshape(top, rows).T
    table = table[jax.random.permutation(jax.random.fold_in(own, 1), rows)]
    offset_by = jax.random.randint(jax.random.fold_in(own, 2), (rows, 1), 0, top)
    return jnp.take_along_axis(table, (jnp.arange(top)[None, :] + offset_by) % top, axis=1)


def load_shares(amount, total, reach, lean, full):
    portions = [(1 << 20) // math.isqrt(grade ** lean) + 1 for grade in range(1, amount + 1)]
    largest = reach if full else min(reach, max(-(-total // amount), total * portions[0] // sum(portions)))
    least = 1 if total - largest >= amount - 1 else 0
    given, rest = [largest] + [least] * (amount - 1), total - largest - least * (amount - 1)
    while rest > 0:
        movable = [i for i in range(1, amount) if given[i] < largest] or [i for i in range(1, amount) if given[i] < reach]
        whole, budget = sum([portions[i] for i in movable]), rest
        for i in movable:
            addition = min(reach - given[i], max(1, budget * portions[i] // whole), rest)
            given[i] = given[i] + addition
            rest = rest - addition
    return np.array(given)


def normal_values(own_key, dims, scale, limit, shards=(), held_as=jnp.bfloat16):
    gain = block_scale(own_key, dims, shards, -0.22, 0.18) if shards else 1.0
    drawn = jax.random.normal(own_key, dims, jnp.float32) * scale * gain
    return jnp.minimum(jnp.maximum(drawn, -limit), limit).astype(held_as)


def setup_inputs(seed: int = 0, part: int = 0) -> dict:
    seeds = jax.random.split(jax.random.key(seed), 10)
    own_keys = jax.random.split(jax.random.fold_in(seeds[9], part), 10)
    patches = normal_values(own_keys[0], (BANDS, SLOTS, P_SIZE, P_SIZE), 1.0, 6.0, ((0, 4), (1, 4)), jnp.float32)
    valid_rows = with_ends(jax.random.randint(own_keys[1], (BANDS, SLOTS), P_SIZE // 4, P_SIZE + 1), jax.random.fold_in(own_keys[1], 1), P_SIZE // 4, P_SIZE).astype(jnp.int32)
    slot_owner_keys = jax.random.split(jax.random.fold_in(own_keys[2], 1), BANDS * SLOTS // SLOTS_DEV)
    slot_owner_turns = jax.random.permutation(jax.random.fold_in(own_keys[2], 3), BANDS * SLOTS // SLOTS_DEV)
    slot_owner = jax.vmap(lambda own, number: shared_out(jax.random.fold_in(own_keys[2], 2), own, number, SLOTS_DEV, N_SKY, 1, CAP, 2))(slot_owner_keys, slot_owner_turns).reshape((BANDS, SLOTS, 1))
    slot_local = with_ends(jax.random.randint(own_keys[3], (BANDS, SLOTS), 0, PATCH_DEV), jax.random.fold_in(own_keys[3], 1), 0, PATCH_DEV - 1).astype(jnp.int32)
    slot_visit = with_ends(jax.random.randint(own_keys[4], (BANDS, SLOTS), 0, VIS), jax.random.fold_in(own_keys[4], 1), 0, VIS - 1).astype(jnp.int32)
    basis_coef = normal_values(own_keys[5], (BANDS, VIS, NB), NB ** -0.5, 1.25, ((0, 4),), jnp.float32)
    inv_var = jnp.clip(jnp.exp(math.log(1.0) - 2.3025851 * jax.random.uniform(own_keys[6], (BANDS, VIS), jnp.float32) ** block_scale(own_keys[6], (BANDS, VIS), ((0, 4),), -0.2, 0.2)), 0.1, 1.0)
    kernel_x = normal_values(seeds[7], (NB, KS), KS ** -0.5, 1.0)
    kernel_y = normal_values(seeds[8], (NB, KS), KS ** -0.5, 1.0)
    return dict(patches=patches, valid_rows=valid_rows, slot_owner=slot_owner, slot_local=slot_local, slot_visit=slot_visit, basis_coef=basis_coef, inv_var=inv_var, kernel_x=kernel_x, kernel_y=kernel_y)


def tables(kernel_x, kernel_y, tile_side):
    kernel_len = kernel_x.shape[1]
    half_len = kernel_len // 2
    row_ids = lax.broadcasted_iota(jnp.int32, (tile_side, tile_side, kernel_len), 0)
    col_ids = lax.broadcasted_iota(jnp.int32, (tile_side, tile_side, kernel_len), 1)
    tap_ids = lax.broadcasted_iota(jnp.int32, (tile_side, tile_side, kernel_len), 2)
    picked = (col_ids - row_ids + half_len == tap_ids).astype(jnp.float32)
    across = jnp.einsum('jma,ka->kjm', picked, kernel_x.astype(jnp.float32), precision=lax.Precision.HIGHEST).astype(jnp.bfloat16)
    down_tables = jnp.einsum('ima,ka->kim', picked, kernel_y.astype(jnp.float32), precision=lax.Precision.HIGHEST).astype(jnp.bfloat16)
    return across, down_tables


def reference(patches, valid_rows, slot_owner, slot_local, slot_visit, basis_coef, inv_var, kernel_x, kernel_y):
    across, down_tables = tables(kernel_x, kernel_y, P_SIZE)
    target = (slot_owner[:, :, 0] * PATCH_DEV + slot_local).astype(jnp.int32)
    row_ids = jnp.arange(P_SIZE, dtype=jnp.int32)

    def one_band(operands):
        band_tiles, row_count, band_target, visits, coef_band, var_band = operands
        kept_rows = row_ids[None, :] < row_count[:, None]
        masked = jnp.where(kept_rows[:, :, None], band_tiles, 0.0).astype(jnp.bfloat16)
        weight = lax.optimization_barrier(var_band[visits].astype(jnp.bfloat16)).astype(jnp.float32)
        coeffs = lax.optimization_barrier(coef_band[visits].astype(jnp.bfloat16)).astype(jnp.float32)
        mixing = lax.optimization_barrier((weight[:, None] * coeffs).astype(jnp.bfloat16)).astype(jnp.float32)
        tiles_wide = masked.astype(jnp.float32)

        def one_basis(basis):
            weighted = mixing[:, basis][:, None, None] * tiles_wide
            return jax.ops.segment_sum(weighted, band_target, num_segments=PATCHES)

        combined = lax.map(one_basis, jnp.arange(NB))
        combined = jnp.transpose(combined, (1, 0, 2, 3)).astype(jnp.bfloat16)
        section_one = jnp.einsum('pkim,kjm->pkij', combined.astype(jnp.float32), across.astype(jnp.float32)).astype(jnp.bfloat16)
        numerator = jnp.einsum('kim,pkmj->pij', down_tables.astype(jnp.float32), section_one.astype(jnp.float32))
        coverage = jax.ops.segment_sum(weight[:, None] * kept_rows.astype(jnp.float32), band_target, num_segments=PATCHES)
        return numerator / jnp.maximum(coverage, 1.0)[:, :, None]

    band_coadd = lax.map(one_band, (patches, valid_rows, target, slot_visit, basis_coef, inv_var))
    detection = jnp.sum(band_coadd, axis=0)
    return band_coadd, detection
```

```python
import functools

import jax
import jax.numpy as jnp
from jax import lax
from jax.experimental import pallas as pl
from jax.experimental.pallas import tpu as pltpu
from jax.sharding import PartitionSpec as P

PATCH_DEV = 8
MESH = pl.DeviceIdType.MESH
F32 = jnp.float32
BF16 = jnp.bfloat16


def chunk_at(t, bands, subs):
    if bands == 1:
        return t * 0, t
    far = (bands - 2) * subs
    near = lax.div(t, far) if far else t * 0 + 1
    pair = lax.rem(t, 2 * subs)
    last = t - far
    offset = (1 - near) * (bands - 1 - 2 * lax.div(t, 2 * subs) - lax.rem(pair, 2))
    offset = offset + near * (1 - lax.div(last, subs))
    return offset, (1 - near) * lax.div(pair, 2) + near * lax.rem(last, subs)


def flip(index, bits, top):
    result = index
    for i in range((top - 1).bit_length()):
        bit = lax.rem(lax.div(bits, 1 << i), 2)
        result = result + (1 << i) * bit * (1 - 2 * lax.rem(lax.div(index, 1 << i), 2))
    return result


def kernel(
    sizes,
    valid_ref,
    owner_ref,
    local_ref,
    visit_ref,
    ivar_ref,
    patches_ref,
    coef_ref,
    kx_ref,
    ky_ref,
    coadd_ref,
    detect_ref,
    raw,
    tiles,
    down,
    across,
    mixed,
    mixing,
    bases,
    results,
    slot_piece,
    meta_send,
    meta_recv,
    x_send,
    x_recv,
    z_recv,
    stage,
    values,
    final,
    det_stage,
    load_sem,
    out_sem,
    det_sem,
    meta_ssem,
    meta_rsem,
    x_ssem,
    x_rsem,
    z_ssem,
    z_rsem,
):
    pieces, side, taps, basis, sky, bands, cap, rows, part, pad = sizes
    half = taps // 2
    window = part + 2 * pad
    me = lax.axis_index("sky")
    band = lax.axis_index("band")
    subs = rows // part
    chunks = bands * subs
    evens = list(range(2, bands, 2))

    def chunk_of(t):
        return chunk_at(jnp.int32(t), bands, subs)

    def band_at(r):
        return flip(band, jnp.int32(r), bands)

    def sky_at(d):
        return lax.rem(me + d, sky)

    barrier = pltpu.get_barrier_semaphore()
    for d in range(1, sky):
        pl.semaphore_signal(barrier, inc=1, device_id={"sky": sky_at(d)}, device_id_type=MESH)
    band_peers = ([1] if bands > 1 else []) + evens
    for r in band_peers:
        pl.semaphore_signal(barrier, inc=1, device_id={"band": band_at(r)}, device_id_type=MESH)

    loads = [
        pltpu.make_async_copy(patches_ref.at[s], raw.at[s], load_sem.at[s]) for s in range(pieces)
    ]
    for load in loads:
        load.start()

    owners = [owner_ref[s] for s in range(pieces)]
    ranks = []
    for s in range(pieces):
        rank = jnp.int32(0)
        for other in range(s):
            rank = rank + (owners[other] == owners[s]).astype(jnp.int32)
        ranks.append(owners[s] * cap + rank)
    tall = -(-basis // 8) * 8
    on_lane = lax.broadcasted_iota(jnp.int32, (tall, basis), 1)
    on_row = lax.broadcasted_iota(jnp.int32, (tall, basis), 0)
    for s in range(pieces):
        weight = jnp.full((1, basis), ivar_ref[visit_ref[s]], F32).astype(BF16).astype(F32)
        coefs = coef_ref[visit_ref[s]].astype(BF16).astype(F32)
        mix = (coefs * weight).astype(BF16).astype(F32)
        column = jnp.sum(
            jnp.where(on_lane == on_row, jnp.broadcast_to(mix, (tall, basis)), 0.0),
            axis=1,
            keepdims=True,
        )
        mixing[s] = jnp.broadcast_to(column, (tall, side))
    for slot in range(sky * cap):
        piece = jnp.int32(0)
        used = jnp.int32(0)
        for s in range(pieces):
            hit = (ranks[s] == slot).astype(jnp.int32)
            piece = piece + hit * s
            used = used + hit
        slot_piece[slot] = piece
        dest, c = divmod(slot, cap)
        meta_send[dest, c : c + 1, :] = (
            jnp.full((1, 128), ivar_ref[visit_ref[piece]], F32).astype(BF16).astype(F32)
        )
        meta_send[dest, cap + c : cap + c + 1, :] = jnp.full(
            (1, 128), valid_ref[piece], jnp.int32
        ).astype(F32)
        meta_send[dest, 2 * cap + c : 2 * cap + c + 1, :] = jnp.full(
            (1, 128), local_ref[piece] * used + used - 1, jnp.int32
        ).astype(F32)
    meta_recv[me] = meta_send[me]

    wide = bases.shape[1]
    taps_at = lax.broadcasted_iota(jnp.int32, (taps, wide), 0) - half
    lanes = lax.broadcasted_iota(jnp.int32, (taps, wide), 1)
    for start, ref, away in ((0, ky_ref, pad + taps_at), (basis, kx_ref, -taps_at)):
        place = (lanes == jnp.where(away < 0, away + wide, away)).astype(BF16)
        bases[start : start + basis, :] = jnp.dot(ref[...], place, preferred_element_type=F32)
    ring_row = lax.broadcasted_iota(jnp.int32, (wide, wide), 0)
    ring_col = lax.broadcasted_iota(jnp.int32, (wide, wide), 1)
    blocks = side // wide

    def make_tables(k, carry):
        row = jnp.broadcast_to(bases[pl.ds(k, 1), :], (part, wide))
        shifted = pltpu.roll(row, 0, 1, stride=1, stride_axis=0)
        down[pl.ds(pl.multiple_of(k * part, part), part), :] = shifted[:, :window].astype(BF16)
        row = jnp.broadcast_to(bases[pl.ds(basis + k, 1), :], (wide, wide))
        ring = pltpu.roll(row, 0, 1, stride=1, stride_axis=0)
        on = jnp.where(jnp.abs(ring_row - ring_col) <= half, ring, 0.0).astype(BF16)
        below = jnp.where(ring_col - ring_row >= wide - half, ring, 0.0).astype(BF16)
        above = jnp.where(ring_row - ring_col >= wide - half, ring, 0.0).astype(BF16)
        none = jnp.zeros((wide, wide), BF16)
        pick = {0: on, 1: below, -1: above}
        for i in range(blocks):
            for j in range(blocks):
                spot = pl.ds(pl.multiple_of(k * side + i * wide, wide), wide)
                across[spot, j * wide : (j + 1) * wide] = pick.get(i - j, none)
        return carry

    lax.fori_loop(0, basis, make_tables, 0)

    row_ids = lax.broadcasted_iota(jnp.int32, (side, side), 0)
    for s in range(pieces):
        tiles[s, 0:pad, :] = jnp.zeros((pad, side), BF16)
        tiles[s, pad + side : side + 2 * pad, :] = jnp.zeros((pad, side), BF16)
        loads[s].wait()
        tiles[s, pad : pad + side, :] = jnp.where(row_ids < valid_ref[s], raw[s], 0.0).astype(BF16)

    def meta_copy(d):
        return pltpu.make_async_remote_copy(
            src_ref=meta_send.at[sky_at(d)],
            dst_ref=meta_recv.at[me],
            send_sem=meta_ssem.at[d],
            recv_sem=meta_rsem.at[d],
            device_id={"sky": sky_at(d)},
            device_id_type=MESH,
        )

    def sky_copy(t, d):
        return pltpu.make_async_remote_copy(
            src_ref=x_send.at[t, sky_at(d)],
            dst_ref=x_recv.at[t, me],
            send_sem=x_ssem.at[t, d],
            recv_sem=x_rsem.at[t, d],
            device_id={"sky": sky_at(d)},
            device_id_type=MESH,
        )

    def band_copy(t, r, source):
        return pltpu.make_async_remote_copy(
            src_ref=source.at[t],
            dst_ref=z_recv.at[t],
            send_sem=z_ssem.at[t],
            recv_sem=z_rsem.at[t],
            device_id={"band": band_at(r)},
            device_id_type=MESH,
        )

    def first_row(t):
        r, sub = chunk_of(t)
        return pl.multiple_of(band_at(r) * rows + sub * part, part)

    def coadd_copy(t):
        return pltpu.make_async_copy(
            final.at[t], coadd_ref.at[:, pl.ds(first_row(t), part), :], out_sem.at[t]
        )

    def detect_copy(sub):
        return pltpu.make_async_copy(
            det_stage.at[sub], detect_ref.at[:, pl.ds(pl.multiple_of(sub * part, part), part), :], det_sem.at[sub]
        )

    def convolve(t):
        rows_in = pl.ds(first_row(t), window)
        for s in range(pieces):
            first = jnp.dot(down[...], tiles[s, rows_in, :], preferred_element_type=F32)
            for k in range(basis):
                scale = jnp.broadcast_to(mixing[s, k : k + 1, :], (part, side))
                mixed[s * part : (s + 1) * part, k * side : (k + 1) * side] = (
                    first[k * part : (k + 1) * part] * scale
                ).astype(BF16)

        def second(_, carry):
            done = jnp.dot(mixed[...], across[...], preferred_element_type=F32)
            results[...] = done.astype(BF16).reshape(pieces, part, side)
            return carry

        once = lax.div(t, chunks) + 1
        lax.fori_loop(0, once, second, 0)

        def to_slots(_, carry):
            for slot in range(sky * cap):
                x_send[t, slot // cap, slot % cap] = results[slot_piece[slot]]
            for c in range(cap):
                x_recv[t, me, c] = results[slot_piece[me * cap + c]]
            return carry

        lax.fori_loop(0, once, to_slots, 0)

        @pl.when(t == 0)
        def _():
            pl.semaphore_wait(barrier, sky - 1 + len(band_peers))
            for d in range(1, sky):
                meta_copy(d).start()

        for d in range(1, sky):
            sky_copy(t, d).start()

    block = 16
    late = lax.rem(me, 2) == 1

    def collect(t):
        r, sub = chunk_of(t)

        @pl.when(t == 0)
        def _():
            for d in range(1, sky):
                meta_copy(d).wait()

        for d in range(1, sky):
            sky_copy(t, d).wait_recv()
        base = first_row(t)

        def some_rows(i, carry):
            spot = pl.ds(pl.multiple_of(i * block, block), block)
            line = lax.broadcasted_iota(jnp.int32, (block, 128), 0) + (base + i * block)
            line = line.astype(F32)
            lane = lax.broadcasted_iota(jnp.int32, (block, 128), 1).astype(F32)
            cover = jnp.zeros((block, 128), F32)
            sums = [jnp.zeros((block, side), F32) for _ in range(PATCH_DEV)]
            for src in range(sky):
                for c in range(cap):
                    weight = meta_recv[src, c : c + 1, :]
                    count = meta_recv[src, cap + c : cap + c + 1, :]
                    local = meta_recv[src, 2 * cap + c : 2 * cap + c + 1, :]
                    cover = cover + jnp.where((lane == local) & (line < count), weight, 0.0)
                    local = jnp.broadcast_to(local[:, :1], (block, side))
                    piece = x_recv[t, src, c, spot, :].astype(F32)
                    for p in range(PATCH_DEV):
                        sums[p] = sums[p] + jnp.where(local == float(p), piece, 0.0)
            scale = 1.0 / jnp.maximum(cover, 1.0)
            for p in range(PATCH_DEV):
                value = sums[p] * jnp.broadcast_to(scale[:, p : p + 1], (block, side))
                final[t, p, spot, :] = value.astype(BF16)
                values[p, spot, :] = value
            return carry

        lax.fori_loop(0, part // block, some_rows, 0)
        coadd_copy(t).start()

        @pl.when(lax.rem(r, 2) == 1)
        def _():
            band_copy(t, 1, final).start()

            @pl.when(late & (t > 0))
            def _():
                before = chunk_of(t - 1)[0]

                @pl.when(lax.rem(before, 2) == 0)
                def _():
                    band_copy(t - 1, before, stage).start()

        @pl.when((lax.rem(r, 2) == 0) & (r > 0))
        def _():
            band_copy(t - 1, 1, final).wait_recv()

            def add(p, carry):
                stage[t, p] = (values[p] + z_recv[t - 1, p].astype(F32)).astype(BF16)
                return carry

            lax.fori_loop(0, PATCH_DEV, add, 0)

            @pl.when(jnp.logical_not(late))
            def _():
                band_copy(t, r, stage).start()

        @pl.when(r == 0)
        def _():
            others = [t - subs] if bands > 1 else []
            for q in evens:
                others.append((bands - 2 - q) * subs + 2 * sub + 1)
            for other in others:
                band_copy(other, 1, final).wait_recv()

            def add(p, carry):
                total = values[p]
                for other in others:
                    total = total + z_recv[other, p].astype(F32)
                det_stage[sub, p] = total.astype(BF16)
                return carry

            lax.fori_loop(0, PATCH_DEV, add, 0)
            detect_copy(sub).start()

    lag = 2

    def step(t, carry):
        @pl.when(t < chunks)
        def _():
            convolve(t)

        @pl.when(t >= lag)
        def _():
            collect(t - lag)

        return carry

    lax.fori_loop(0, chunks + lag, step, 0)

    def finish(t, carry):
        r, sub = chunk_of(t)
        for d in range(1, sky):
            sky_copy(t, d).wait_send()
        coadd_copy(t).wait()

        @pl.when(r > 0)
        def _():
            band_copy(t, 1, final).wait_send()

        @pl.when(r == 0)
        def _():
            detect_copy(sub).wait()

        return carry

    lax.fori_loop(0, chunks, finish, 0)


def widen(coadd_in, detect_in, coadd_out, detect_out, coadd_a, detect_a, coadd_b, detect_b, in_sem, out_sem):
    pairs = ((coadd_in, coadd_a, coadd_b, coadd_out), (detect_in, detect_a, detect_b, detect_out))
    loads, stores = [], []
    for p in range(PATCH_DEV):
        for which, (source, narrow, wide, dest) in enumerate(pairs):
            loads.append(pltpu.make_async_copy(source.at[p], narrow.at[p], in_sem.at[which, p]))
            stores.append(pltpu.make_async_copy(wide.at[p], dest.at[p], out_sem.at[which, p]))
    for load in loads:
        load.start()
    for p in range(PATCH_DEV):
        for which, (source, narrow, wide, dest) in enumerate(pairs):
            loads[2 * p + which].wait()
            wide[p] = narrow[p].astype(F32)
            stores[2 * p + which].start()
    for store in stores:
        store.wait()


def per_device(
    patches, valid_rows, slot_owner, slot_local, slot_visit, basis_coef, inv_var, kernel_x, kernel_y
):
    pieces, side = patches.shape[1], patches.shape[2]
    basis, taps = kernel_x.shape
    sky, bands = lax.axis_size("sky"), lax.axis_size("band")
    cap = max(2, 2 * pieces // sky)
    rows = side // bands
    part = min(rows, 32)
    pad = -(-(taps // 2) // 16) * 16
    chunks = side // part
    meta_rows = -(-3 * cap // 8) * 8
    smem = pl.BlockSpec(memory_space=pltpu.SMEM)
    vmem = pl.BlockSpec(memory_space=pltpu.VMEM)
    hbm = pl.BlockSpec(memory_space=pl.ANY)
    sizes = (pieces, side, taps, basis, sky, bands, cap, rows, part, pad)
    coadd, detection = pl.pallas_call(
        functools.partial(kernel, sizes),
        out_shape=(
            jax.ShapeDtypeStruct((PATCH_DEV, side, side), BF16),
            jax.ShapeDtypeStruct((PATCH_DEV, rows, side), BF16),
        ),
        in_specs=[smem] * 5 + [hbm, vmem, vmem, vmem],
        out_specs=(hbm, hbm),
        scratch_shapes=[
            pltpu.VMEM((pieces, side, side), F32),
            pltpu.VMEM((pieces, side + 2 * pad, side), BF16),
            pltpu.VMEM((basis * part, part + 2 * pad), BF16),
            pltpu.VMEM((basis * side, side), BF16),
            pltpu.VMEM((pieces * part, basis * side), BF16),
            pltpu.VMEM((pieces, -(-basis // 8) * 8, side), F32),
            pltpu.VMEM((2 * basis, 128), F32),
            pltpu.VMEM((pieces, part, side), BF16),
            pltpu.SMEM((sky * cap,), jnp.int32),
            pltpu.VMEM((sky, meta_rows, 128), F32),
            pltpu.VMEM((sky, meta_rows, 128), F32),
            pltpu.VMEM((chunks, sky, cap, part, side), BF16),
            pltpu.VMEM((chunks, sky, cap, part, side), BF16),
            pltpu.VMEM((chunks, PATCH_DEV, part, side), BF16),
            pltpu.VMEM((chunks, PATCH_DEV, part, side), BF16),
            pltpu.VMEM((PATCH_DEV, part, side), F32),
            pltpu.VMEM((chunks, PATCH_DEV, part, side), BF16),
            pltpu.VMEM((rows // part, PATCH_DEV, part, side), BF16),
            pltpu.SemaphoreType.DMA((pieces,)),
            pltpu.SemaphoreType.DMA((chunks,)),
            pltpu.SemaphoreType.DMA((rows // part,)),
            pltpu.SemaphoreType.DMA((sky,)),
            pltpu.SemaphoreType.DMA((sky,)),
            pltpu.SemaphoreType.DMA((chunks, sky)),
            pltpu.SemaphoreType.DMA((chunks, sky)),
            pltpu.SemaphoreType.DMA((chunks,)),
            pltpu.SemaphoreType.DMA((chunks,)),
        ],
        compiler_params=pltpu.CompilerParams(
            collective_id=0, has_side_effects=True, vmem_limit_bytes=60 * 1024 * 1024
        ),
    )(
        valid_rows[0],
        slot_owner[0, :, 0],
        slot_local[0],
        slot_visit[0],
        inv_var[0],
        patches[0],
        jnp.transpose(basis_coef, (1, 0, 2)),
        kernel_x,
        kernel_y,
    )
    coadd, detection = pl.pallas_call(
        widen,
        out_shape=(
            jax.ShapeDtypeStruct(coadd.shape, F32),
            jax.ShapeDtypeStruct(detection.shape, F32),
        ),
        in_specs=[hbm, hbm],
        out_specs=(hbm, hbm),
        scratch_shapes=[
            pltpu.VMEM(coadd.shape, BF16),
            pltpu.VMEM(detection.shape, BF16),
            pltpu.VMEM(coadd.shape, F32),
            pltpu.VMEM(detection.shape, F32),
            pltpu.SemaphoreType.DMA((2, PATCH_DEV)),
            pltpu.SemaphoreType.DMA((2, PATCH_DEV)),
        ],
    )(coadd, detection)
    return coadd[None], detection


def solution(mesh):
    in_specs = (
        P(("tract", "band"), "sky", None, None),
        P(("tract", "band"), "sky"),
        P(("tract", "band"), "sky", None),
        P(("tract", "band"), "sky"),
        P(("tract", "band"), "sky"),
        P(("tract", "band"), None, None),
        P(("tract", "band"), None),
        P(),
        P(),
    )
    out_specs = (P(("tract", "band"), "sky", None, None), P(("tract", "sky"), "band", None))
    return jax.shard_map(
        per_device, mesh=mesh, in_specs=in_specs, out_specs=out_specs, check_vma=False
    )
```

```python
import functools

import jax
import jax.numpy as jnp
from jax import lax
from jax.experimental import pallas as pl
from jax.experimental.pallas import tpu as pltpu
from jax.sharding import PartitionSpec as P

PATCH_DEV = 8
MESH = pl.DeviceIdType.MESH
F32 = jnp.float32
BF16 = jnp.bfloat16


def chunk_at(t, bands, subs):
    if bands == 1:
        return t * 0, t
    far = (bands - 2) * subs
    near = lax.div(t, far) if far else t * 0 + 1
    pair = lax.rem(t, 2 * subs)
    last = t - far
    offset = (1 - near) * (bands - 1 - 2 * lax.div(t, 2 * subs) - lax.rem(pair, 2))
    offset = offset + near * (1 - lax.div(last, subs))
    return offset, (1 - near) * lax.div(pair, 2) + near * lax.rem(last, subs)


def flip(index, bits, top):
    result = index
    for i in range((top - 1).bit_length()):
        bit = lax.rem(lax.div(bits, 1 << i), 2)
        result = result + (1 << i) * bit * (1 - 2 * lax.rem(lax.div(index, 1 << i), 2))
    return result


def kernel(
    sizes,
    valid_ref,
    owner_ref,
    local_ref,
    visit_ref,
    ivar_ref,
    patches_ref,
    coef_ref,
    kx_ref,
    ky_ref,
    coadd_ref,
    detect_ref,
    raw,
    tiles,
    down,
    across,
    mixed,
    mixing,
    bases,
    results,
    slot_piece,
    meta_send,
    meta_recv,
    x_send,
    x_recv,
    z_recv,
    stage,
    values,
    final,
    det_stage,
    load_sem,
    out_sem,
    det_sem,
    meta_ssem,
    meta_rsem,
    x_ssem,
    x_rsem,
    z_ssem,
    z_rsem,
):
    pieces, side, taps, basis, sky, bands, cap, rows, part, pad = sizes
    half = taps // 2
    window = part + 2 * pad
    me = lax.axis_index("sky")
    band = lax.axis_index("band")
    subs = rows // part
    chunks = bands * subs
    evens = list(range(2, bands, 2))

    def chunk_of(t):
        return chunk_at(jnp.int32(t), bands, subs)

    def band_at(r):
        return flip(band, jnp.int32(r), bands)

    def sky_at(d):
        return lax.rem(me + d, sky)

    barrier = pltpu.get_barrier_semaphore()
    for d in range(1, sky):
        pl.semaphore_signal(barrier, inc=1, device_id={"sky": sky_at(d)}, device_id_type=MESH)
    odd = lax.rem(band, 2)

    def up(r):
        return lax.div(band_at(r) - band - 1 + bands, bands)

    def outer(r):
        return up(r) * (1 - odd) + (1 - up(r)) * odd

    greeted = jnp.int32(sky - 1)
    for r in range(1, bands):

        def greet(r=r):
            pl.semaphore_signal(
                barrier, inc=1, device_id={"band": band_at(r)}, device_id_type=MESH
            )

        if r % 2 and r > 1:
            pl.when(outer(r) == 0)(greet)
            greeted = greeted + 1 - outer(r)
        else:
            greet()
            greeted = greeted + 1

    loads = [
        pltpu.make_async_copy(patches_ref.at[s], raw.at[s], load_sem.at[s]) for s in range(pieces)
    ]
    for load in loads:
        load.start()

    owners = [owner_ref[s] for s in range(pieces)]
    ranks = []
    for s in range(pieces):
        rank = jnp.int32(0)
        for other in range(s):
            rank = rank + (owners[other] == owners[s]).astype(jnp.int32)
        ranks.append(owners[s] * cap + rank)
    tall = -(-basis // 8) * 8
    on_lane = lax.broadcasted_iota(jnp.int32, (tall, basis), 1)
    on_row = lax.broadcasted_iota(jnp.int32, (tall, basis), 0)
    for s in range(pieces):
        weight = jnp.full((1, basis), ivar_ref[visit_ref[s]], F32).astype(BF16).astype(F32)
        coefs = coef_ref[visit_ref[s]].astype(BF16).astype(F32)
        mix = (coefs * weight).astype(BF16).astype(F32)
        column = jnp.sum(
            jnp.where(on_lane == on_row, jnp.broadcast_to(mix, (tall, basis)), 0.0),
            axis=1,
            keepdims=True,
        )
        mixing[s] = jnp.broadcast_to(column, (tall, side))
    for slot in range(sky * cap):
        piece = jnp.int32(0)
        used = jnp.int32(0)
        for s in range(pieces):
            hit = (ranks[s] == slot).astype(jnp.int32)
            piece = piece + hit * s
            used = used + hit
        slot_piece[slot] = piece
        dest, c = divmod(slot, cap)
        meta_send[dest, c : c + 1, :] = (
            jnp.full((1, 128), ivar_ref[visit_ref[piece]], F32).astype(BF16).astype(F32)
        )
        meta_send[dest, cap + c : cap + c + 1, :] = jnp.full(
            (1, 128), valid_ref[piece], jnp.int32
        ).astype(F32)
        meta_send[dest, 2 * cap + c : 2 * cap + c + 1, :] = jnp.full(
            (1, 128), local_ref[piece] * used + used - 1, jnp.int32
        ).astype(F32)
    meta_recv[me] = meta_send[me]

    wide = bases.shape[1]
    taps_at = lax.broadcasted_iota(jnp.int32, (taps, wide), 0) - half
    lanes = lax.broadcasted_iota(jnp.int32, (taps, wide), 1)
    for start, ref, away in ((0, ky_ref, pad + taps_at), (basis, kx_ref, -taps_at)):
        place = (lanes == jnp.where(away < 0, away + wide, away)).astype(BF16)
        bases[start : start + basis, :] = jnp.dot(ref[...], place, preferred_element_type=F32)
    ring_row = lax.broadcasted_iota(jnp.int32, (wide, wide), 0)
    ring_col = lax.broadcasted_iota(jnp.int32, (wide, wide), 1)
    blocks = side // wide

    def make_tables(k, carry):
        row = jnp.broadcast_to(bases[pl.ds(k, 1), :], (part, wide))
        shifted = pltpu.roll(row, 0, 1, stride=1, stride_axis=0)
        down[pl.ds(pl.multiple_of(k * part, part), part), :] = shifted[:, :window].astype(BF16)
        row = jnp.broadcast_to(bases[pl.ds(basis + k, 1), :], (wide, wide))
        ring = pltpu.roll(row, 0, 1, stride=1, stride_axis=0)
        on = jnp.where(jnp.abs(ring_row - ring_col) <= half, ring, 0.0).astype(BF16)
        below = jnp.where(ring_col - ring_row >= wide - half, ring, 0.0).astype(BF16)
        above = jnp.where(ring_row - ring_col >= wide - half, ring, 0.0).astype(BF16)
        none = jnp.zeros((wide, wide), BF16)
        pick = {0: on, 1: below, -1: above}
        for i in range(blocks):
            for j in range(blocks):
                spot = pl.ds(pl.multiple_of(k * side + i * wide, wide), wide)
                across[spot, j * wide : (j + 1) * wide] = pick.get(i - j, none)
        return carry

    lax.fori_loop(0, basis, make_tables, 0)

    row_ids = lax.broadcasted_iota(jnp.int32, (side, side), 0)
    for s in range(pieces):
        tiles[s, 0:pad, :] = jnp.zeros((pad, side), BF16)
        tiles[s, pad + side : side + 2 * pad, :] = jnp.zeros((pad, side), BF16)
        loads[s].wait()
        tiles[s, pad : pad + side, :] = jnp.where(row_ids < valid_ref[s], raw[s], 0.0).astype(BF16)

    def meta_copy(d):
        return pltpu.make_async_remote_copy(
            src_ref=meta_send.at[sky_at(d)],
            dst_ref=meta_recv.at[me],
            send_sem=meta_ssem.at[d],
            recv_sem=meta_rsem.at[d],
            device_id={"sky": sky_at(d)},
            device_id_type=MESH,
        )

    def sky_copy(t, d):
        return pltpu.make_async_remote_copy(
            src_ref=x_send.at[t, sky_at(d)],
            dst_ref=x_recv.at[t, me],
            send_sem=x_ssem.at[t, d],
            recv_sem=x_rsem.at[t, d],
            device_id={"sky": sky_at(d)},
            device_id_type=MESH,
        )

    def band_copy(t, r, source, hop):
        return pltpu.make_async_remote_copy(
            src_ref=source.at[t],
            dst_ref=z_recv.at[hop, t],
            send_sem=z_ssem.at[t],
            recv_sem=z_rsem.at[hop, t],
            device_id={"band": band_at(r)},
            device_id_type=MESH,
        )

    def first_row(t):
        r, sub = chunk_of(t)
        return pl.multiple_of(band_at(r) * rows + sub * part, part)

    def coadd_copy(t):
        return pltpu.make_async_copy(
            final.at[t], coadd_ref.at[:, pl.ds(first_row(t), part), :], out_sem.at[t]
        )

    def detect_copy(sub):
        return pltpu.make_async_copy(
            det_stage.at[sub], detect_ref.at[:, pl.ds(pl.multiple_of(sub * part, part), part), :], det_sem.at[sub]
        )

    def convolve(t):
        rows_in = pl.ds(first_row(t), window)
        for s in range(pieces):
            first = jnp.dot(down[...], tiles[s, rows_in, :], preferred_element_type=F32)
            for k in range(basis):
                scale = jnp.broadcast_to(mixing[s, k : k + 1, :], (part, side))
                mixed[s * part : (s + 1) * part, k * side : (k + 1) * side] = (
                    first[k * part : (k + 1) * part] * scale
                ).astype(BF16)

        def second(_, carry):
            done = jnp.dot(mixed[...], across[...], preferred_element_type=F32)
            results[...] = done.astype(BF16).reshape(pieces, part, side)
            return carry

        once = lax.div(t, chunks) + 1
        lax.fori_loop(0, once, second, 0)

        def to_slots(_, carry):
            for slot in range(sky * cap):
                x_send[t, slot // cap, slot % cap] = results[slot_piece[slot]]
            for c in range(cap):
                x_recv[t, me, c] = results[slot_piece[me * cap + c]]
            return carry

        lax.fori_loop(0, once, to_slots, 0)

        @pl.when(t == 0)
        def _():
            pl.semaphore_wait(barrier, greeted)
            for d in range(1, sky):
                meta_copy(d).start()

        for d in range(1, sky):
            sky_copy(t, d).start()

    block = 16
    def collect(t):
        r, sub = chunk_of(t)

        @pl.when(t == 0)
        def _():
            for d in range(1, sky):
                meta_copy(d).wait()

        for d in range(1, sky):
            sky_copy(t, d).wait_recv()
        base = first_row(t)

        def some_rows(i, carry):
            spot = pl.ds(pl.multiple_of(i * block, block), block)
            line = lax.broadcasted_iota(jnp.int32, (block, 128), 0) + (base + i * block)
            line = line.astype(F32)
            lane = lax.broadcasted_iota(jnp.int32, (block, 128), 1).astype(F32)
            cover = jnp.zeros((block, 128), F32)
            sums = [jnp.zeros((block, side), F32) for _ in range(PATCH_DEV)]
            for src in range(sky):
                for c in range(cap):
                    weight = meta_recv[src, c : c + 1, :]
                    count = meta_recv[src, cap + c : cap + c + 1, :]
                    local = meta_recv[src, 2 * cap + c : 2 * cap + c + 1, :]
                    cover = cover + jnp.where((lane == local) & (line < count), weight, 0.0)
                    local = jnp.broadcast_to(local[:, :1], (block, side))
                    piece = x_recv[t, src, c, spot, :].astype(F32)
                    for p in range(PATCH_DEV):
                        sums[p] = sums[p] + jnp.where(local == float(p), piece, 0.0)
            scale = 1.0 / jnp.maximum(cover, 1.0)
            for p in range(PATCH_DEV):
                value = sums[p] * jnp.broadcast_to(scale[:, p : p + 1], (block, side))
                final[t, p, spot, :] = value.astype(BF16)
                values[lax.rem(t, 4), p, spot, :] = value
            return carry

        lax.fori_loop(0, part // block, some_rows, 0)
        coadd_copy(t).start()

        @pl.when((r == 1) | ((r > 1) & (outer(r) == 1)))
        def _():
            band_copy(t, 1, final, 0).start()

        @pl.when(r == 0)
        def _():
            others = [(0, t - subs)] if bands > 1 else []
            for q in evens:
                through = up(q) * odd + (1 - up(q)) * (1 - odd)
                others.append((1, (bands - 2 - q) * subs + 2 * sub + 1 - through))
            for hop, other in others:
                band_copy(other, 1, final, hop).wait_recv()

            def add(p, carry):
                total = values[lax.rem(t, 4), p]
                for hop, other in others:
                    total = total + z_recv[hop, other, p].astype(F32)
                det_stage[sub, p] = total.astype(BF16)
                return carry

            lax.fori_loop(0, PATCH_DEV, add, 0)
            detect_copy(sub).start()

    def forward(t, other):
        r = chunk_of(t)[0]

        @pl.when(outer(r) == 0)
        def _():
            band_copy(other, 1, final, 0).wait_recv()

            def add(p, carry):
                near = values[lax.rem(t, 4), p]
                stage[t, p] = (near + z_recv[0, other, p].astype(F32)).astype(BF16)
                return carry

            lax.fori_loop(0, PATCH_DEV, add, 0)
            band_copy(t, r, stage, 1).start()

    far = (bands - 2) * subs

    def forwards(t):
        if far <= 0:
            return

        @pl.when((lax.rem(t, 2) == 0) & (t >= 2) & (t <= far))
        def _():
            forward(t - 1, t - 2)

        @pl.when((lax.rem(t, 2) == 1) & (t >= 3) & (t <= far + 1))
        def _():
            forward(t - 3, t - 2)

    lag = 2

    def step(t, carry):
        @pl.when(t < chunks)
        def _():
            convolve(t)

        @pl.when(t >= lag)
        def _():
            collect(t - lag)
            forwards(t - lag)

        return carry

    lax.fori_loop(0, chunks + lag, step, 0)

    def finish(t, carry):
        r, sub = chunk_of(t)
        for d in range(1, sky):
            sky_copy(t, d).wait_send()
        coadd_copy(t).wait()

        @pl.when(r > 0)
        def _():
            band_copy(t, 1, final, 0).wait_send()

        @pl.when(r == 0)
        def _():
            detect_copy(sub).wait()

        return carry

    lax.fori_loop(0, chunks, finish, 0)


def widen(coadd_in, detect_in, coadd_out, detect_out, coadd_a, detect_a, coadd_b, detect_b, in_sem, out_sem):
    pairs = ((coadd_in, coadd_a, coadd_b, coadd_out), (detect_in, detect_a, detect_b, detect_out))
    loads, stores = [], []
    for p in range(PATCH_DEV):
        for which, (source, narrow, wide, dest) in enumerate(pairs):
            loads.append(pltpu.make_async_copy(source.at[p], narrow.at[p], in_sem.at[which, p]))
            stores.append(pltpu.make_async_copy(wide.at[p], dest.at[p], out_sem.at[which, p]))
    for load in loads:
        load.start()
    for p in range(PATCH_DEV):
        for which, (source, narrow, wide, dest) in enumerate(pairs):
            loads[2 * p + which].wait()
            wide[p] = narrow[p].astype(F32)
            stores[2 * p + which].start()
    for store in stores:
        store.wait()


def per_device(
    patches, valid_rows, slot_owner, slot_local, slot_visit, basis_coef, inv_var, kernel_x, kernel_y
):
    pieces, side = patches.shape[1], patches.shape[2]
    basis, taps = kernel_x.shape
    sky, bands = lax.axis_size("sky"), lax.axis_size("band")
    cap = max(2, 2 * pieces // sky)
    rows = side // bands
    part = min(rows, 32)
    pad = -(-(taps // 2) // 16) * 16
    chunks = side // part
    meta_rows = -(-3 * cap // 8) * 8
    smem = pl.BlockSpec(memory_space=pltpu.SMEM)
    vmem = pl.BlockSpec(memory_space=pltpu.VMEM)
    hbm = pl.BlockSpec(memory_space=pl.ANY)
    sizes = (pieces, side, taps, basis, sky, bands, cap, rows, part, pad)
    coadd, detection = pl.pallas_call(
        functools.partial(kernel, sizes),
        out_shape=(
            jax.ShapeDtypeStruct((PATCH_DEV, side, side), BF16),
            jax.ShapeDtypeStruct((PATCH_DEV, rows, side), BF16),
        ),
        in_specs=[smem] * 5 + [hbm, vmem, vmem, vmem],
        out_specs=(hbm, hbm),
        scratch_shapes=[
            pltpu.VMEM((pieces, side, side), F32),
            pltpu.VMEM((pieces, side + 2 * pad, side), BF16),
            pltpu.VMEM((basis * part, part + 2 * pad), BF16),
            pltpu.VMEM((basis * side, side), BF16),
            pltpu.VMEM((pieces * part, basis * side), BF16),
            pltpu.VMEM((pieces, -(-basis // 8) * 8, side), F32),
            pltpu.VMEM((2 * basis, 128), F32),
            pltpu.VMEM((pieces, part, side), BF16),
            pltpu.SMEM((sky * cap,), jnp.int32),
            pltpu.VMEM((sky, meta_rows, 128), F32),
            pltpu.VMEM((sky, meta_rows, 128), F32),
            pltpu.VMEM((chunks, sky, cap, part, side), BF16),
            pltpu.VMEM((chunks, sky, cap, part, side), BF16),
            pltpu.VMEM((2, chunks, PATCH_DEV, part, side), BF16),
            pltpu.VMEM((chunks, PATCH_DEV, part, side), BF16),
            pltpu.VMEM((4, PATCH_DEV, part, side), F32),
            pltpu.VMEM((chunks, PATCH_DEV, part, side), BF16),
            pltpu.VMEM((rows // part, PATCH_DEV, part, side), BF16),
            pltpu.SemaphoreType.DMA((pieces,)),
            pltpu.SemaphoreType.DMA((chunks,)),
            pltpu.SemaphoreType.DMA((rows // part,)),
            pltpu.SemaphoreType.DMA((sky,)),
            pltpu.SemaphoreType.DMA((sky,)),
            pltpu.SemaphoreType.DMA((chunks, sky)),
            pltpu.SemaphoreType.DMA((chunks, sky)),
            pltpu.SemaphoreType.DMA((chunks,)),
            pltpu.SemaphoreType.DMA((2, chunks)),
        ],
        compiler_params=pltpu.CompilerParams(
            collective_id=0, has_side_effects=True, vmem_limit_bytes=60 * 1024 * 1024
        ),
    )(
        valid_rows[0],
        slot_owner[0, :, 0],
        slot_local[0],
        slot_visit[0],
        inv_var[0],
        patches[0],
        jnp.transpose(basis_coef, (1, 0, 2)),
        kernel_x,
        kernel_y,
    )
    coadd, detection = pl.pallas_call(
        widen,
        out_shape=(
            jax.ShapeDtypeStruct(coadd.shape, F32),
            jax.ShapeDtypeStruct(detection.shape, F32),
        ),
        in_specs=[hbm, hbm],
        out_specs=(hbm, hbm),
        scratch_shapes=[
            pltpu.VMEM(coadd.shape, BF16),
            pltpu.VMEM(detection.shape, BF16),
            pltpu.VMEM(coadd.shape, F32),
            pltpu.VMEM(detection.shape, F32),
            pltpu.SemaphoreType.DMA((2, PATCH_DEV)),
            pltpu.SemaphoreType.DMA((2, PATCH_DEV)),
        ],
    )(coadd, detection)
    return coadd[None], detection


def solution(mesh):
    in_specs = (
        P(("tract", "band"), "sky", None, None),
        P(("tract", "band"), "sky"),
        P(("tract", "band"), "sky", None),
        P(("tract", "band"), "sky"),
        P(("tract", "band"), "sky"),
        P(("tract", "band"), None, None),
        P(("tract", "band"), None),
        P(),
        P(),
    )
    out_specs = (P(("tract", "band"), "sky", None, None), P(("tract", "sky"), "band", None))
    return jax.shard_map(
        per_device, mesh=mesh, in_specs=in_specs, out_specs=out_specs, check_vma=False
    )
```

```python
import functools

import jax
import jax.numpy as jnp
from jax import lax
from jax.experimental import pallas as pl
from jax.experimental.pallas import tpu as pltpu
from jax.sharding import PartitionSpec as P

PATCH_DEV = 8
MESH = pl.DeviceIdType.MESH
F32 = jnp.float32
BF16 = jnp.bfloat16


def chunk_at(t, bands, subs):
    if bands == 1:
        return t * 0, t
    far = (bands - 2) * subs
    near = lax.div(t, far) if far else t * 0 + 1
    pair = lax.rem(t, 2 * subs)
    last = t - far
    offset = (1 - near) * (bands - 1 - 2 * lax.div(t, 2 * subs) - lax.rem(pair, 2))
    offset = offset + near * (1 - lax.div(last, subs))
    return offset, (1 - near) * lax.div(pair, 2) + near * lax.rem(last, subs)


def flip(index, bits, top):
    result = index
    for i in range((top - 1).bit_length()):
        bit = lax.rem(lax.div(bits, 1 << i), 2)
        result = result + (1 << i) * bit * (1 - 2 * lax.rem(lax.div(index, 1 << i), 2))
    return result


def kernel(
    sizes,
    valid_ref,
    owner_ref,
    local_ref,
    visit_ref,
    ivar_ref,
    patches_ref,
    coef_ref,
    kx_ref,
    ky_ref,
    coadd_ref,
    detect_ref,
    raw,
    tiles,
    down,
    across,
    mixed,
    mixing,
    bases,
    results,
    slot_piece,
    meta_send,
    meta_recv,
    x_send,
    x_recv,
    z_recv,
    stage,
    values,
    final,
    load_sem,
    meta_ssem,
    meta_rsem,
    x_ssem,
    x_rsem,
    z_ssem,
    z_rsem,
):
    pieces, side, taps, basis, sky, bands, cap, rows, part, pad = sizes
    half = taps // 2
    window = part + 2 * pad
    me = lax.axis_index("sky")
    band = lax.axis_index("band")
    subs = rows // part
    chunks = bands * subs
    evens = list(range(2, bands, 2))

    def chunk_of(t):
        return chunk_at(jnp.int32(t), bands, subs)

    def band_at(r):
        return flip(band, jnp.int32(r), bands)

    def sky_at(d):
        return lax.rem(me + d, sky)

    barrier = pltpu.get_barrier_semaphore()
    for d in range(1, sky):
        pl.semaphore_signal(barrier, inc=1, device_id={"sky": sky_at(d)}, device_id_type=MESH)
    odd = lax.rem(band, 2)

    def up(r):
        return lax.div(band_at(r) - band - 1 + bands, bands)

    def outer(r):
        return up(r) * (1 - odd) + (1 - up(r)) * odd

    greeted = jnp.int32(sky - 1)
    for r in range(1, bands):

        def greet(r=r):
            pl.semaphore_signal(
                barrier, inc=1, device_id={"band": band_at(r)}, device_id_type=MESH
            )

        if r % 2 and r > 1:
            pl.when(outer(r) == 0)(greet)
            greeted = greeted + 1 - outer(r)
        else:
            greet()
            greeted = greeted + 1

    loads = [
        pltpu.make_async_copy(patches_ref.at[s], raw.at[s], load_sem.at[s]) for s in range(pieces)
    ]
    for load in loads:
        load.start()

    owners = [owner_ref[s] for s in range(pieces)]
    ranks = []
    for s in range(pieces):
        rank = jnp.int32(0)
        for other in range(s):
            rank = rank + (owners[other] == owners[s]).astype(jnp.int32)
        ranks.append(owners[s] * cap + rank)
    tall = -(-basis // 8) * 8
    on_lane = lax.broadcasted_iota(jnp.int32, (tall, basis), 1)
    on_row = lax.broadcasted_iota(jnp.int32, (tall, basis), 0)
    for s in range(pieces):
        weight = jnp.full((1, basis), ivar_ref[visit_ref[s]], F32).astype(BF16).astype(F32)
        coefs = coef_ref[visit_ref[s]].astype(BF16).astype(F32)
        mix = (coefs * weight).astype(BF16).astype(F32)
        column = jnp.sum(
            jnp.where(on_lane == on_row, jnp.broadcast_to(mix, (tall, basis)), 0.0),
            axis=1,
            keepdims=True,
        )
        mixing[s] = jnp.broadcast_to(column, (tall, side))
    for slot in range(sky * cap):
        piece = jnp.int32(0)
        used = jnp.int32(0)
        for s in range(pieces):
            hit = (ranks[s] == slot).astype(jnp.int32)
            piece = piece + hit * s
            used = used + hit
        slot_piece[slot] = piece
        dest, c = divmod(slot, cap)
        meta_send[dest, c : c + 1, :] = (
            jnp.full((1, 128), ivar_ref[visit_ref[piece]], F32).astype(BF16).astype(F32)
        )
        meta_send[dest, cap + c : cap + c + 1, :] = jnp.full(
            (1, 128), valid_ref[piece], jnp.int32
        ).astype(F32)
        meta_send[dest, 2 * cap + c : 2 * cap + c + 1, :] = jnp.full(
            (1, 128), local_ref[piece] * used + used - 1, jnp.int32
        ).astype(F32)
    meta_recv[me] = meta_send[me]

    wide = bases.shape[1]
    taps_at = lax.broadcasted_iota(jnp.int32, (taps, wide), 0) - half
    lanes = lax.broadcasted_iota(jnp.int32, (taps, wide), 1)
    for start, ref, away in ((0, ky_ref, pad + taps_at), (basis, kx_ref, -taps_at)):
        place = (lanes == jnp.where(away < 0, away + wide, away)).astype(BF16)
        bases[start : start + basis, :] = jnp.dot(ref[...], place, preferred_element_type=F32)
    ring_row = lax.broadcasted_iota(jnp.int32, (wide, wide), 0)
    ring_col = lax.broadcasted_iota(jnp.int32, (wide, wide), 1)
    blocks = side // wide

    def make_tables(k, carry):
        row = jnp.broadcast_to(bases[pl.ds(k, 1), :], (part, wide))
        shifted = pltpu.roll(row, 0, 1, stride=1, stride_axis=0)
        down[pl.ds(pl.multiple_of(k * part, part), part), :] = shifted[:, :window].astype(BF16)
        row = jnp.broadcast_to(bases[pl.ds(basis + k, 1), :], (wide, wide))
        ring = pltpu.roll(row, 0, 1, stride=1, stride_axis=0)
        on = jnp.where(jnp.abs(ring_row - ring_col) <= half, ring, 0.0).astype(BF16)
        below = jnp.where(ring_col - ring_row >= wide - half, ring, 0.0).astype(BF16)
        above = jnp.where(ring_row - ring_col >= wide - half, ring, 0.0).astype(BF16)
        none = jnp.zeros((wide, wide), BF16)
        pick = {0: on, 1: below, -1: above}
        for i in range(blocks):
            for j in range(blocks):
                spot = pl.ds(pl.multiple_of(k * side + i * wide, wide), wide)
                across[spot, j * wide : (j + 1) * wide] = pick.get(i - j, none)
        return carry

    lax.fori_loop(0, basis, make_tables, 0)

    row_ids = lax.broadcasted_iota(jnp.int32, (side, side), 0)
    for s in range(pieces):
        tiles[s, 0:pad, :] = jnp.zeros((pad, side), BF16)
        tiles[s, pad + side : side + 2 * pad, :] = jnp.zeros((pad, side), BF16)
        loads[s].wait()
        tiles[s, pad : pad + side, :] = jnp.where(row_ids < valid_ref[s], raw[s], 0.0).astype(BF16)

    def meta_copy(d):
        return pltpu.make_async_remote_copy(
            src_ref=meta_send.at[sky_at(d)],
            dst_ref=meta_recv.at[me],
            send_sem=meta_ssem.at[d],
            recv_sem=meta_rsem.at[d],
            device_id={"sky": sky_at(d)},
            device_id_type=MESH,
        )

    def sky_copy(t, d):
        return pltpu.make_async_remote_copy(
            src_ref=x_send.at[t, sky_at(d)],
            dst_ref=x_recv.at[t, me],
            send_sem=x_ssem.at[t, d],
            recv_sem=x_rsem.at[t, d],
            device_id={"sky": sky_at(d)},
            device_id_type=MESH,
        )

    def band_copy(t, r, source, hop):
        return pltpu.make_async_remote_copy(
            src_ref=source.at[t],
            dst_ref=z_recv.at[hop, t],
            send_sem=z_ssem.at[t],
            recv_sem=z_rsem.at[hop, t],
            device_id={"band": band_at(r)},
            device_id_type=MESH,
        )

    def first_row(t):
        r, sub = chunk_of(t)
        return pl.multiple_of(band_at(r) * rows + sub * part, part)

    def convolve(t):
        rows_in = pl.ds(first_row(t), window)
        for s in range(pieces):
            first = jnp.dot(down[...], tiles[s, rows_in, :], preferred_element_type=F32)
            for k in range(basis):
                scale = jnp.broadcast_to(mixing[s, k : k + 1, :], (part, side))
                mixed[s * part : (s + 1) * part, k * side : (k + 1) * side] = (
                    first[k * part : (k + 1) * part] * scale
                ).astype(BF16)

        def second(_, carry):
            done = jnp.dot(mixed[...], across[...], preferred_element_type=F32)
            results[...] = done.astype(BF16).reshape(pieces, part, side)
            return carry

        once = lax.div(t, chunks) + 1
        lax.fori_loop(0, once, second, 0)

        def to_slots(_, carry):
            for slot in range(sky * cap):
                x_send[t, slot // cap, slot % cap] = results[slot_piece[slot]]
            for c in range(cap):
                x_recv[t, me, c] = results[slot_piece[me * cap + c]]
            return carry

        lax.fori_loop(0, once, to_slots, 0)

        @pl.when(t == 0)
        def _():
            pl.semaphore_wait(barrier, greeted)
            for d in range(1, sky):
                meta_copy(d).start()

        for d in range(1, sky):
            sky_copy(t, d).start()

    block = 16
    def collect(t):
        r, sub = chunk_of(t)

        @pl.when(t == 0)
        def _():
            for d in range(1, sky):
                meta_copy(d).wait()

        for d in range(1, sky):
            sky_copy(t, d).wait_recv()
        base = first_row(t)

        def some_rows(i, carry):
            spot = pl.ds(pl.multiple_of(i * block, block), block)
            line = lax.broadcasted_iota(jnp.int32, (block, 128), 0) + (base + i * block)
            line = line.astype(F32)
            lane = lax.broadcasted_iota(jnp.int32, (block, 128), 1).astype(F32)
            cover = jnp.zeros((block, 128), F32)
            sums = [jnp.zeros((block, side), F32) for _ in range(PATCH_DEV)]
            for src in range(sky):
                for c in range(cap):
                    weight = meta_recv[src, c : c + 1, :]
                    count = meta_recv[src, cap + c : cap + c + 1, :]
                    local = meta_recv[src, 2 * cap + c : 2 * cap + c + 1, :]
                    cover = cover + jnp.where((lane == local) & (line < count), weight, 0.0)
                    local = jnp.broadcast_to(local[:, :1], (block, side))
                    piece = x_recv[t, src, c, spot, :].astype(F32)
                    for p in range(PATCH_DEV):
                        sums[p] = sums[p] + jnp.where(local == float(p), piece, 0.0)
            scale = 1.0 / jnp.maximum(cover, 1.0)
            for p in range(PATCH_DEV):
                value = sums[p] * jnp.broadcast_to(scale[:, p : p + 1], (block, side))
                final[t, p, spot, :] = value.astype(BF16)
                coadd_ref[p, pl.ds(pl.multiple_of(base + i * block, block), block), :] = value
                values[lax.rem(t, 4), p, spot, :] = value
            return carry

        lax.fori_loop(0, part // block, some_rows, 0)

        @pl.when((r == 1) | ((r > 1) & (outer(r) == 1)))
        def _():
            band_copy(t, 1, final, 0).start()

        @pl.when(r == 0)
        def _():
            others = [(0, t - subs)] if bands > 1 else []
            for q in evens:
                through = up(q) * odd + (1 - up(q)) * (1 - odd)
                others.append((1, (bands - 2 - q) * subs + 2 * sub + 1 - through))
            for hop, other in others:
                band_copy(other, 1, final, hop).wait_recv()

            def add(p, carry):
                total = values[lax.rem(t, 4), p]
                for hop, other in others:
                    total = total + z_recv[hop, other, p].astype(F32)
                detect_ref[p, pl.ds(pl.multiple_of(sub * part, part), part), :] = total
                return carry

            lax.fori_loop(0, PATCH_DEV, add, 0)

    def forward(t, other):
        r = chunk_of(t)[0]

        @pl.when(outer(r) == 0)
        def _():
            band_copy(other, 1, final, 0).wait_recv()

            def add(p, carry):
                near = values[lax.rem(t, 4), p]
                stage[t, p] = (near + z_recv[0, other, p].astype(F32)).astype(BF16)
                return carry

            lax.fori_loop(0, PATCH_DEV, add, 0)
            band_copy(t, r, stage, 1).start()

    far = (bands - 2) * subs

    def forwards(t):
        if far <= 0:
            return

        @pl.when((lax.rem(t, 2) == 0) & (t >= 2) & (t <= far))
        def _():
            forward(t - 1, t - 2)

        @pl.when((lax.rem(t, 2) == 1) & (t >= 3) & (t <= far + 1))
        def _():
            forward(t - 3, t - 2)

    lag = 3

    def step(t, carry):
        @pl.when(t < chunks)
        def _():
            convolve(t)

        @pl.when(t >= lag)
        def _():
            collect(t - lag)
            forwards(t - lag)

        return carry

    lax.fori_loop(0, chunks + lag, step, 0)

    def finish(t, carry):
        r = chunk_of(t)[0]
        for d in range(1, sky):
            sky_copy(t, d).wait_send()

        @pl.when(r > 0)
        def _():
            band_copy(t, 1, final, 0).wait_send()

        return carry

    lax.fori_loop(0, chunks, finish, 0)


def put(coadd_in, detect_in, coadd_out, detect_out, sem):
    copies = [
        pltpu.make_async_copy(coadd_in.at[p], coadd_out.at[p], sem.at[p]) for p in range(PATCH_DEV)
    ]
    copies.append(pltpu.make_async_copy(detect_in, detect_out, sem.at[PATCH_DEV]))
    for copy in copies:
        copy.start()
    for copy in copies:
        copy.wait()


def per_device(
    patches, valid_rows, slot_owner, slot_local, slot_visit, basis_coef, inv_var, kernel_x, kernel_y
):
    pieces, side = patches.shape[1], patches.shape[2]
    basis, taps = kernel_x.shape
    sky, bands = lax.axis_size("sky"), lax.axis_size("band")
    cap = max(2, 2 * pieces // sky)
    rows = side // bands
    part = min(rows, 16)
    pad = -(-(taps // 2) // 16) * 16
    chunks = side // part
    meta_rows = -(-3 * cap // 8) * 8
    smem = pl.BlockSpec(memory_space=pltpu.SMEM)
    vmem = pl.BlockSpec(memory_space=pltpu.VMEM)
    hbm = pl.BlockSpec(memory_space=pl.ANY)
    sizes = (pieces, side, taps, basis, sky, bands, cap, rows, part, pad)
    coadd, detection = pl.pallas_call(
        functools.partial(kernel, sizes),
        out_shape=(
            pltpu.VMEM((PATCH_DEV, side, side), F32),
            pltpu.VMEM((PATCH_DEV, rows, side), F32),
        ),
        in_specs=[smem] * 5 + [hbm, vmem, vmem, vmem],
        out_specs=(vmem, vmem),
        scratch_shapes=[
            pltpu.VMEM((pieces, side, side), F32),
            pltpu.VMEM((pieces, side + 2 * pad, side), BF16),
            pltpu.VMEM((basis * part, part + 2 * pad), BF16),
            pltpu.VMEM((basis * side, side), BF16),
            pltpu.VMEM((pieces * part, basis * side), BF16),
            pltpu.VMEM((pieces, -(-basis // 8) * 8, side), F32),
            pltpu.VMEM((2 * basis, 128), F32),
            pltpu.VMEM((pieces, part, side), BF16),
            pltpu.SMEM((sky * cap,), jnp.int32),
            pltpu.VMEM((sky, meta_rows, 128), F32),
            pltpu.VMEM((sky, meta_rows, 128), F32),
            pltpu.VMEM((chunks, sky, cap, part, side), BF16),
            pltpu.VMEM((chunks, sky, cap, part, side), BF16),
            pltpu.VMEM((2, chunks, PATCH_DEV, part, side), BF16),
            pltpu.VMEM((chunks, PATCH_DEV, part, side), BF16),
            pltpu.VMEM((4, PATCH_DEV, part, side), F32),
            pltpu.VMEM((chunks, PATCH_DEV, part, side), BF16),
            pltpu.SemaphoreType.DMA((pieces,)),
            pltpu.SemaphoreType.DMA((sky,)),
            pltpu.SemaphoreType.DMA((sky,)),
            pltpu.SemaphoreType.DMA((chunks, sky)),
            pltpu.SemaphoreType.DMA((chunks, sky)),
            pltpu.SemaphoreType.DMA((chunks,)),
            pltpu.SemaphoreType.DMA((2, chunks)),
        ],
        compiler_params=pltpu.CompilerParams(
            collective_id=0, has_side_effects=True, vmem_limit_bytes=60 * 1024 * 1024
        ),
    )(
        valid_rows[0],
        slot_owner[0, :, 0],
        slot_local[0],
        slot_visit[0],
        inv_var[0],
        patches[0],
        jnp.transpose(basis_coef, (1, 0, 2)),
        kernel_x,
        kernel_y,
    )
    in_vmem = pltpu.MemorySpace.VMEM
    coadd, detection = pl.pallas_call(
        put,
        out_shape=(
            jax.ShapeDtypeStruct(coadd.shape, F32),
            jax.ShapeDtypeStruct(detection.shape, F32),
        ),
        in_specs=[vmem, vmem],
        out_specs=(hbm, hbm),
        scratch_shapes=[pltpu.SemaphoreType.DMA((PATCH_DEV + 1,))],
        compiler_params=pltpu.CompilerParams(vmem_limit_bytes=1024 * 1024),
    )(
        pltpu.with_memory_space_constraint(coadd, in_vmem),
        pltpu.with_memory_space_constraint(detection, in_vmem),
    )
    return coadd[None], detection


def solution(mesh):
    in_specs = (
        P(("tract", "band"), "sky", None, None),
        P(("tract", "band"), "sky"),
        P(("tract", "band"), "sky", None),
        P(("tract", "band"), "sky"),
        P(("tract", "band"), "sky"),
        P(("tract", "band"), None, None),
        P(("tract", "band"), None),
        P(),
        P(),
    )
    out_specs = (P(("tract", "band"), "sky", None, None), P(("tract", "sky"), "band", None))
    return jax.shard_map(
        per_device, mesh=mesh, in_specs=in_specs, out_specs=out_specs, check_vma=False
    )
```

```python
import functools

import jax
import jax.numpy as jnp
from jax import lax
from jax.experimental import pallas as pl
from jax.experimental.pallas import tpu as pltpu
from jax.sharding import PartitionSpec as P

PATCH_DEV = 8
MESH = pl.DeviceIdType.MESH
F32 = jnp.float32
BF16 = jnp.bfloat16


def chunk_at(t, bands, subs):
    if bands == 1:
        return t * 0, t
    far = (bands - 2) * subs
    near = lax.div(t, far) if far else t * 0 + 1
    pair = lax.rem(t, 2 * subs)
    last = t - far
    offset = (1 - near) * (bands - 1 - 2 * lax.div(t, 2 * subs) - lax.rem(pair, 2))
    offset = offset + near * (1 - lax.div(last, subs))
    return offset, (1 - near) * lax.div(pair, 2) + near * lax.rem(last, subs)


def flip(index, bits, top):
    result = index
    for i in range((top - 1).bit_length()):
        bit = lax.rem(lax.div(bits, 1 << i), 2)
        result = result + (1 << i) * bit * (1 - 2 * lax.rem(lax.div(index, 1 << i), 2))
    return result


def kernel(
    sizes,
    valid_ref,
    owner_ref,
    local_ref,
    visit_ref,
    ivar_ref,
    patches_ref,
    coef_ref,
    kx_ref,
    ky_ref,
    coadd_ref,
    detect_ref,
    raw,
    tiles,
    down,
    across,
    mixed,
    mixing,
    bases,
    results,
    slot_piece,
    meta_send,
    meta_recv,
    x_send,
    x_recv,
    z_recv,
    stage,
    values,
    final,
    load_sem,
    meta_ssem,
    meta_rsem,
    x_ssem,
    x_rsem,
    z_ssem,
    z_rsem,
):
    pieces, side, taps, basis, sky, bands, cap, rows, part, pad = sizes
    half = taps // 2
    window = part + 2 * pad
    me = lax.axis_index("sky")
    band = lax.axis_index("band")
    subs = rows // part
    chunks = bands * subs
    evens = list(range(2, bands, 2))

    def chunk_of(t):
        return chunk_at(jnp.int32(t), bands, subs)

    def band_at(r):
        return flip(band, jnp.int32(r), bands)

    def sky_at(d):
        return lax.rem(me + d, sky)

    barrier = pltpu.get_barrier_semaphore()
    for d in range(1, sky):
        pl.semaphore_signal(barrier, inc=1, device_id={"sky": sky_at(d)}, device_id_type=MESH)
    odd = lax.rem(band, 2)

    def up(r):
        return lax.div(band_at(r) - band - 1 + bands, bands)

    def outer(r):
        return up(r) * (1 - odd) + (1 - up(r)) * odd

    greeted = jnp.int32(sky - 1)
    for r in range(1, bands):

        def greet(r=r):
            pl.semaphore_signal(
                barrier, inc=1, device_id={"band": band_at(r)}, device_id_type=MESH
            )

        if r % 2 and r > 1:
            pl.when(outer(r) == 0)(greet)
            greeted = greeted + 1 - outer(r)
        else:
            greet()
            greeted = greeted + 1

    loads = [
        pltpu.make_async_copy(patches_ref.at[s], raw.at[s], load_sem.at[s]) for s in range(pieces)
    ]
    for load in loads:
        load.start()

    owners = [owner_ref[s] for s in range(pieces)]
    ranks = []
    for s in range(pieces):
        rank = jnp.int32(0)
        for other in range(s):
            rank = rank + (owners[other] == owners[s]).astype(jnp.int32)
        ranks.append(owners[s] * cap + rank)
    tall = -(-basis // 8) * 8
    on_lane = lax.broadcasted_iota(jnp.int32, (tall, basis), 1)
    on_row = lax.broadcasted_iota(jnp.int32, (tall, basis), 0)
    for s in range(pieces):
        weight = jnp.full((1, basis), ivar_ref[visit_ref[s]], F32).astype(BF16).astype(F32)
        coefs = coef_ref[visit_ref[s]].astype(BF16).astype(F32)
        mix = (coefs * weight).astype(BF16).astype(F32)
        column = jnp.sum(
            jnp.where(on_lane == on_row, jnp.broadcast_to(mix, (tall, basis)), 0.0),
            axis=1,
            keepdims=True,
        )
        mixing[s] = jnp.broadcast_to(column, (tall, side))
    for slot in range(sky * cap):
        piece = jnp.int32(0)
        used = jnp.int32(0)
        for s in range(pieces):
            hit = (ranks[s] == slot).astype(jnp.int32)
            piece = piece + hit * s
            used = used + hit
        slot_piece[slot] = piece
        dest, c = divmod(slot, cap)
        meta_send[dest, c : c + 1, :] = (
            jnp.full((1, 128), ivar_ref[visit_ref[piece]], F32).astype(BF16).astype(F32)
        )
        meta_send[dest, cap + c : cap + c + 1, :] = jnp.full(
            (1, 128), valid_ref[piece], jnp.int32
        ).astype(F32)
        meta_send[dest, 2 * cap + c : 2 * cap + c + 1, :] = jnp.full(
            (1, 128), local_ref[piece] * used + used - 1, jnp.int32
        ).astype(F32)
    meta_recv[me] = meta_send[me]

    wide = bases.shape[1]
    taps_at = lax.broadcasted_iota(jnp.int32, (taps, wide), 0) - half
    lanes = lax.broadcasted_iota(jnp.int32, (taps, wide), 1)
    for start, ref, away in ((0, ky_ref, pad + taps_at), (basis, kx_ref, -taps_at)):
        place = (lanes == jnp.where(away < 0, away + wide, away)).astype(BF16)
        bases[start : start + basis, :] = jnp.dot(ref[...], place, preferred_element_type=F32)
    ring_row = lax.broadcasted_iota(jnp.int32, (wide, wide), 0)
    ring_col = lax.broadcasted_iota(jnp.int32, (wide, wide), 1)
    blocks = side // wide

    def make_tables(k, carry):
        row = jnp.broadcast_to(bases[pl.ds(k, 1), :], (part, wide))
        shifted = pltpu.roll(row, 0, 1, stride=1, stride_axis=0)
        down[pl.ds(pl.multiple_of(k * part, part), part), :] = shifted[:, :window].astype(BF16)
        row = jnp.broadcast_to(bases[pl.ds(basis + k, 1), :], (wide, wide))
        ring = pltpu.roll(row, 0, 1, stride=1, stride_axis=0)
        on = jnp.where(jnp.abs(ring_row - ring_col) <= half, ring, 0.0).astype(BF16)
        edge = -(-half // 16) * 16
        rest = jnp.zeros((wide - edge, wide), BF16)
        top = jnp.where(ring_col[:edge] - ring_row[:edge] >= wide - half, ring[:edge], 0.0)
        below = jnp.concatenate([top.astype(BF16), rest], axis=0)
        low = wide - edge
        end = jnp.where(ring_row[low:] - ring_col[low:] >= wide - half, ring[low:], 0.0)
        above = jnp.concatenate([rest, end.astype(BF16)], axis=0)
        none = jnp.zeros((wide, wide), BF16)
        pick = {0: on, 1: below, -1: above}
        for i in range(blocks):
            for j in range(blocks):
                spot = pl.ds(pl.multiple_of(k * side + i * wide, wide), wide)
                across[spot, j * wide : (j + 1) * wide] = pick.get(i - j, none)
        return carry

    lax.fori_loop(0, basis, make_tables, 0, unroll=3)

    row_ids = lax.broadcasted_iota(jnp.int32, (side, side), 0)
    for s in range(pieces):
        tiles[s, 0:pad, :] = jnp.zeros((pad, side), BF16)
        tiles[s, pad + side : side + 2 * pad, :] = jnp.zeros((pad, side), BF16)
        loads[s].wait()
        tiles[s, pad : pad + side, :] = jnp.where(row_ids < valid_ref[s], raw[s], 0.0).astype(BF16)

    def meta_copy(d):
        return pltpu.make_async_remote_copy(
            src_ref=meta_send.at[sky_at(d)],
            dst_ref=meta_recv.at[me],
            send_sem=meta_ssem.at[d],
            recv_sem=meta_rsem.at[d],
            device_id={"sky": sky_at(d)},
            device_id_type=MESH,
        )

    def sky_copy(t, d):
        return pltpu.make_async_remote_copy(
            src_ref=x_send.at[t, sky_at(d)],
            dst_ref=x_recv.at[t, me],
            send_sem=x_ssem.at[t, d],
            recv_sem=x_rsem.at[t, d],
            device_id={"sky": sky_at(d)},
            device_id_type=MESH,
        )

    def band_copy(t, r, source, hop):
        return pltpu.make_async_remote_copy(
            src_ref=source.at[t],
            dst_ref=z_recv.at[hop, t],
            send_sem=z_ssem.at[t],
            recv_sem=z_rsem.at[hop, t],
            device_id={"band": band_at(r)},
            device_id_type=MESH,
        )

    def first_row(t):
        r, sub = chunk_of(t)
        return pl.multiple_of(band_at(r) * rows + sub * part, part)

    def convolve(t):
        rows_in = pl.ds(first_row(t), window)
        for s in range(pieces):
            first = jnp.dot(down[...], tiles[s, rows_in, :], preferred_element_type=F32)
            for k in range(basis):
                scale = jnp.broadcast_to(mixing[s, k : k + 1, :], (part, side))
                mixed[s * part : (s + 1) * part, k * side : (k + 1) * side] = (
                    first[k * part : (k + 1) * part] * scale
                ).astype(BF16)

        def second(_, carry):
            done = jnp.dot(mixed[...], across[...], preferred_element_type=F32)
            results[...] = done.astype(BF16).reshape(pieces, part, side)
            return carry

        once = lax.div(t, chunks) + 1
        lax.fori_loop(0, once, second, 0)

        def to_slots(_, carry):
            for slot in range(sky * cap):
                x_send[t, slot // cap, slot % cap] = results[slot_piece[slot]]
            for c in range(cap):
                x_recv[t, me, c] = results[slot_piece[me * cap + c]]
            return carry

        lax.fori_loop(0, once, to_slots, 0)

        @pl.when(t == 0)
        def _():
            pl.semaphore_wait(barrier, greeted)
            for d in range(1, sky):
                meta_copy(d).start()

        for d in range(1, sky):
            sky_copy(t, d).start()

    block = 16
    def collect(t):
        r, sub = chunk_of(t)

        @pl.when(t == 0)
        def _():
            for d in range(1, sky):
                meta_copy(d).wait()

        for d in range(1, sky):
            sky_copy(t, d).wait_recv()
        base = first_row(t)

        def some_rows(i, carry):
            spot = pl.ds(pl.multiple_of(i * block, block), block)
            line = lax.broadcasted_iota(jnp.int32, (block, 128), 0) + (base + i * block)
            line = line.astype(F32)
            lane = lax.broadcasted_iota(jnp.int32, (block, 128), 1).astype(F32)
            cover = jnp.zeros((block, 128), F32)
            sums = [jnp.zeros((block, side), F32) for _ in range(PATCH_DEV)]
            for src in range(sky):
                for c in range(cap):
                    weight = meta_recv[src, c : c + 1, :]
                    count = meta_recv[src, cap + c : cap + c + 1, :]
                    local = meta_recv[src, 2 * cap + c : 2 * cap + c + 1, :]
                    cover = cover + jnp.where((lane == local) & (line < count), weight, 0.0)
                    local = jnp.broadcast_to(local[:, :1], (block, side))
                    piece = x_recv[t, src, c, spot, :].astype(F32)
                    for p in range(PATCH_DEV):
                        sums[p] = sums[p] + jnp.where(local == float(p), piece, 0.0)
            scale = 1.0 / jnp.maximum(cover, 1.0)
            for p in range(PATCH_DEV):
                value = sums[p] * jnp.broadcast_to(scale[:, p : p + 1], (block, side))
                final[t, p, spot, :] = value.astype(BF16)
                coadd_ref[p, pl.ds(pl.multiple_of(base + i * block, block), block), :] = value
                values[lax.rem(t, 4), p, spot, :] = value
            return carry

        lax.fori_loop(0, part // block, some_rows, 0)

        @pl.when((r == 1) | ((r > 1) & (outer(r) == 1)))
        def _():
            band_copy(t, 1, final, 0).start()

        @pl.when(r == 0)
        def _():
            others = [(0, t - subs)] if bands > 1 else []
            for q in evens:
                through = up(q) * odd + (1 - up(q)) * (1 - odd)
                others.append((1, (bands - 2 - q) * subs + 2 * sub + 1 - through))
            for hop, other in others:
                band_copy(other, 1, final, hop).wait_recv()

            def add(p, carry):
                total = values[lax.rem(t, 4), p]
                for hop, other in others:
                    total = total + z_recv[hop, other, p].astype(F32)
                detect_ref[p, pl.ds(pl.multiple_of(sub * part, part), part), :] = total
                return carry

            lax.fori_loop(0, PATCH_DEV, add, 0)

    def forward(t, other):
        r = chunk_of(t)[0]

        @pl.when(outer(r) == 0)
        def _():
            band_copy(other, 1, final, 0).wait_recv()

            def add(p, carry):
                near = values[lax.rem(t, 4), p]
                stage[t, p] = (near + z_recv[0, other, p].astype(F32)).astype(BF16)
                return carry

            lax.fori_loop(0, PATCH_DEV, add, 0)
            band_copy(t, r, stage, 1).start()

    far = (bands - 2) * subs

    def forwards(t):
        if far <= 0:
            return

        @pl.when((lax.rem(t, 2) == 0) & (t >= 2) & (t <= far))
        def _():
            forward(t - 1, t - 2)

        @pl.when((lax.rem(t, 2) == 1) & (t >= 3) & (t <= far + 1))
        def _():
            forward(t - 3, t - 2)

    lag = 3

    def step(t, carry):
        @pl.when(t < chunks)
        def _():
            convolve(t)

        @pl.when(t >= lag)
        def _():
            collect(t - lag)
            forwards(t - lag)

        return carry

    lax.fori_loop(0, chunks + lag, step, 0)

    def finish(t, carry):
        r = chunk_of(t)[0]
        for d in range(1, sky):
            sky_copy(t, d).wait_send()

        @pl.when(r > 0)
        def _():
            band_copy(t, 1, final, 0).wait_send()

        return carry

    lax.fori_loop(0, chunks, finish, 0)


def put(coadd_in, detect_in, coadd_out, detect_out, sem):
    copies = [
        pltpu.make_async_copy(coadd_in.at[p], coadd_out.at[p], sem.at[p]) for p in range(PATCH_DEV)
    ]
    copies.append(pltpu.make_async_copy(detect_in, detect_out, sem.at[PATCH_DEV]))
    for copy in copies:
        copy.start()
    for copy in copies:
        copy.wait()


def per_device(
    patches, valid_rows, slot_owner, slot_local, slot_visit, basis_coef, inv_var, kernel_x, kernel_y
):
    pieces, side = patches.shape[1], patches.shape[2]
    basis, taps = kernel_x.shape
    sky, bands = lax.axis_size("sky"), lax.axis_size("band")
    cap = max(2, 2 * pieces // sky)
    rows = side // bands
    part = min(rows, 16)
    pad = -(-(taps // 2) // 16) * 16
    chunks = side // part
    meta_rows = -(-3 * cap // 8) * 8
    smem = pl.BlockSpec(memory_space=pltpu.SMEM)
    vmem = pl.BlockSpec(memory_space=pltpu.VMEM)
    hbm = pl.BlockSpec(memory_space=pl.ANY)
    sizes = (pieces, side, taps, basis, sky, bands, cap, rows, part, pad)
    coadd, detection = pl.pallas_call(
        functools.partial(kernel, sizes),
        out_shape=(
            pltpu.VMEM((PATCH_DEV, side, side), F32),
            pltpu.VMEM((PATCH_DEV, rows, side), F32),
        ),
        in_specs=[smem] * 5 + [hbm, vmem, vmem, vmem],
        out_specs=(vmem, vmem),
        scratch_shapes=[
            pltpu.VMEM((pieces, side, side), F32),
            pltpu.VMEM((pieces, side + 2 * pad, side), BF16),
            pltpu.VMEM((basis * part, part + 2 * pad), BF16),
            pltpu.VMEM((basis * side, side), BF16),
            pltpu.VMEM((pieces * part, basis * side), BF16),
            pltpu.VMEM((pieces, -(-basis // 8) * 8, side), F32),
            pltpu.VMEM((2 * basis, 128), F32),
            pltpu.VMEM((pieces, part, side), BF16),
            pltpu.SMEM((sky * cap,), jnp.int32),
            pltpu.VMEM((sky, meta_rows, 128), F32),
            pltpu.VMEM((sky, meta_rows, 128), F32),
            pltpu.VMEM((chunks, sky, cap, part, side), BF16),
            pltpu.VMEM((chunks, sky, cap, part, side), BF16),
            pltpu.VMEM((2, chunks, PATCH_DEV, part, side), BF16),
            pltpu.VMEM((chunks, PATCH_DEV, part, side), BF16),
            pltpu.VMEM((4, PATCH_DEV, part, side), F32),
            pltpu.VMEM((chunks, PATCH_DEV, part, side), BF16),
            pltpu.SemaphoreType.DMA((pieces,)),
            pltpu.SemaphoreType.DMA((sky,)),
            pltpu.SemaphoreType.DMA((sky,)),
            pltpu.SemaphoreType.DMA((chunks, sky)),
            pltpu.SemaphoreType.DMA((chunks, sky)),
            pltpu.SemaphoreType.DMA((chunks,)),
            pltpu.SemaphoreType.DMA((2, chunks)),
        ],
        compiler_params=pltpu.CompilerParams(
            collective_id=0, has_side_effects=True, vmem_limit_bytes=60 * 1024 * 1024
        ),
    )(
        valid_rows[0],
        slot_owner[0, :, 0],
        slot_local[0],
        slot_visit[0],
        inv_var[0],
        patches[0],
        jnp.transpose(basis_coef, (1, 0, 2)),
        kernel_x,
        kernel_y,
    )
    in_vmem = pltpu.MemorySpace.VMEM
    coadd, detection = pl.pallas_call(
        put,
        out_shape=(
            jax.ShapeDtypeStruct(coadd.shape, F32),
            jax.ShapeDtypeStruct(detection.shape, F32),
        ),
        in_specs=[vmem, vmem],
        out_specs=(hbm, hbm),
        scratch_shapes=[pltpu.SemaphoreType.DMA((PATCH_DEV + 1,))],
        compiler_params=pltpu.CompilerParams(vmem_limit_bytes=1024 * 1024),
    )(
        pltpu.with_memory_space_constraint(coadd, in_vmem),
        pltpu.with_memory_space_constraint(detection, in_vmem),
    )
    return coadd[None], detection


def solution(mesh):
    in_specs = (
        P(("tract", "band"), "sky", None, None),
        P(("tract", "band"), "sky"),
        P(("tract", "band"), "sky", None),
        P(("tract", "band"), "sky"),
        P(("tract", "band"), "sky"),
        P(("tract", "band"), None, None),
        P(("tract", "band"), None),
        P(),
        P(),
    )
    out_specs = (P(("tract", "band"), "sky", None, None), P(("tract", "sky"), "band", None))
    return jax.shard_map(
        per_device, mesh=mesh, in_specs=in_specs, out_specs=out_specs, check_vma=False
    )
```

```python
import functools

import jax
import jax.numpy as jnp
from jax import lax
from jax.experimental import pallas as pl
from jax.experimental.pallas import tpu as pltpu
from jax.sharding import PartitionSpec as P

PATCH_DEV = 8
MESH = pl.DeviceIdType.MESH
F32 = jnp.float32
BF16 = jnp.bfloat16


def chunk_at(t, bands, subs):
    if bands == 1:
        return t * 0, t
    far = (bands - 2) * subs
    near = lax.div(t, far) if far else t * 0 + 1
    pair = lax.rem(t, 2 * subs)
    last = t - far
    offset = (1 - near) * (bands - 1 - 2 * lax.div(t, 2 * subs) - lax.rem(pair, 2))
    offset = offset + near * (1 - lax.div(last, subs))
    return offset, (1 - near) * lax.div(pair, 2) + near * lax.rem(last, subs)


def flip(index, bits, top):
    result = index
    for i in range((top - 1).bit_length()):
        bit = lax.rem(lax.div(bits, 1 << i), 2)
        result = result + (1 << i) * bit * (1 - 2 * lax.rem(lax.div(index, 1 << i), 2))
    return result


def kernel(
    sizes,
    valid_ref,
    owner_ref,
    local_ref,
    visit_ref,
    ivar_ref,
    patches_ref,
    coef_ref,
    kx_ref,
    ky_ref,
    coadd_ref,
    detect_ref,
    raw,
    tiles,
    down,
    across,
    mixed,
    mixing,
    bases,
    results,
    slot_piece,
    meta_send,
    meta_recv,
    x_send,
    x_recv,
    z_recv,
    stage,
    values,
    final,
    load_sem,
    meta_ssem,
    meta_rsem,
    x_ssem,
    x_rsem,
    z_ssem,
    z_rsem,
):
    pieces, side, taps, basis, sky, bands, cap, rows, part, pad = sizes
    half = taps // 2
    window = part + 2 * pad
    me = lax.axis_index("sky")
    band = lax.axis_index("band")
    subs = rows // part
    chunks = bands * subs
    evens = list(range(2, bands, 2))

    def chunk_of(t):
        return chunk_at(jnp.int32(t), bands, subs)

    def band_at(r):
        return flip(band, jnp.int32(r), bands)

    def sky_at(d):
        return lax.rem(me + d, sky)

    loads = [
        pltpu.make_async_copy(patches_ref.at[s], raw.at[s], load_sem.at[s]) for s in range(pieces)
    ]
    for load in loads:
        load.start()

    barrier = pltpu.get_barrier_semaphore()
    for d in range(1, sky):
        pl.semaphore_signal(barrier, inc=1, device_id={"sky": sky_at(d)}, device_id_type=MESH)
    odd = lax.rem(band, 2)

    def up(r):
        return lax.div(band_at(r) - band - 1 + bands, bands)

    def outer(r):
        return up(r) * (1 - odd) + (1 - up(r)) * odd

    greeted = jnp.int32(sky - 1)
    for r in range(1, bands):

        def greet(r=r):
            pl.semaphore_signal(
                barrier, inc=1, device_id={"band": band_at(r)}, device_id_type=MESH
            )

        if r % 2 and r > 1:
            pl.when(outer(r) == 0)(greet)
            greeted = greeted + 1 - outer(r)
        else:
            greet()
            greeted = greeted + 1

    wide = bases.shape[1]
    taps_at = lax.broadcasted_iota(jnp.int32, (taps, wide), 0) - half
    lanes = lax.broadcasted_iota(jnp.int32, (taps, wide), 1)
    for start, ref, away in ((0, ky_ref, pad + taps_at), (basis, kx_ref, -taps_at)):
        place = (lanes == jnp.where(away < 0, away + wide, away)).astype(BF16)
        bases[start : start + basis, :] = jnp.dot(ref[...], place, preferred_element_type=F32)
    ring_row = lax.broadcasted_iota(jnp.int32, (wide, wide), 0)
    ring_col = lax.broadcasted_iota(jnp.int32, (wide, wide), 1)
    blocks = side // wide

    def make_tables(k, carry):
        row = jnp.broadcast_to(bases[pl.ds(k, 1), :], (part, wide))
        shifted = pltpu.roll(row, 0, 1, stride=1, stride_axis=0)
        down[pl.ds(pl.multiple_of(k * part, part), part), :] = shifted[:, :window].astype(BF16)
        row = jnp.broadcast_to(bases[pl.ds(basis + k, 1), :], (wide, wide))
        ring = pltpu.roll(row, 0, 1, stride=1, stride_axis=0)
        on = jnp.where(jnp.abs(ring_row - ring_col) <= half, ring, 0.0).astype(BF16)
        edge = -(-half // 16) * 16
        rest = jnp.zeros((wide - edge, wide), BF16)
        top = jnp.where(ring_col[:edge] - ring_row[:edge] >= wide - half, ring[:edge], 0.0)
        below = jnp.concatenate([top.astype(BF16), rest], axis=0)
        low = wide - edge
        end = jnp.where(ring_row[low:] - ring_col[low:] >= wide - half, ring[low:], 0.0)
        above = jnp.concatenate([rest, end.astype(BF16)], axis=0)
        none = jnp.zeros((wide, wide), BF16)
        pick = {0: on, 1: below, -1: above}
        for i in range(blocks):
            for j in range(blocks):
                spot = pl.ds(pl.multiple_of(k * side + i * wide, wide), wide)
                across[spot, j * wide : (j + 1) * wide] = pick.get(i - j, none)
        return carry

    lax.fori_loop(0, basis, make_tables, 0, unroll=3)

    owners = [owner_ref[s] for s in range(pieces)]
    ranks = []
    for s in range(pieces):
        rank = jnp.int32(0)
        for other in range(s):
            rank = rank + (owners[other] == owners[s]).astype(jnp.int32)
        ranks.append(owners[s] * cap + rank)
    tall = -(-basis // 8) * 8
    on_lane = lax.broadcasted_iota(jnp.int32, (tall, basis), 1)
    on_row = lax.broadcasted_iota(jnp.int32, (tall, basis), 0)
    for s in range(pieces):
        weight = jnp.full((1, basis), ivar_ref[visit_ref[s]], F32).astype(BF16).astype(F32)
        coefs = coef_ref[visit_ref[s]].astype(BF16).astype(F32)
        mix = (coefs * weight).astype(BF16).astype(F32)
        column = jnp.sum(
            jnp.where(on_lane == on_row, jnp.broadcast_to(mix, (tall, basis)), 0.0),
            axis=1,
            keepdims=True,
        )
        mixing[s] = jnp.broadcast_to(column, (tall, side))
    for slot in range(sky * cap):
        piece = jnp.int32(0)
        used = jnp.int32(0)
        for s in range(pieces):
            hit = (ranks[s] == slot).astype(jnp.int32)
            piece = piece + hit * s
            used = used + hit
        slot_piece[slot] = piece
        dest, c = divmod(slot, cap)
        meta_send[dest, c : c + 1, :] = (
            jnp.full((1, 128), ivar_ref[visit_ref[piece]], F32).astype(BF16).astype(F32)
        )
        meta_send[dest, cap + c : cap + c + 1, :] = jnp.full(
            (1, 128), valid_ref[piece], jnp.int32
        ).astype(F32)
        meta_send[dest, 2 * cap + c : 2 * cap + c + 1, :] = jnp.full(
            (1, 128), local_ref[piece] * used + used - 1, jnp.int32
        ).astype(F32)
    meta_recv[me] = meta_send[me]

    row_ids = lax.broadcasted_iota(jnp.int32, (side, side), 0)
    for s in range(pieces):
        tiles[s, 0:pad, :] = jnp.zeros((pad, side), BF16)
        tiles[s, pad + side : side + 2 * pad, :] = jnp.zeros((pad, side), BF16)
        loads[s].wait()
        tiles[s, pad : pad + side, :] = jnp.where(row_ids < valid_ref[s], raw[s], 0.0).astype(BF16)

    def meta_copy(d):
        return pltpu.make_async_remote_copy(
            src_ref=meta_send.at[sky_at(d)],
            dst_ref=meta_recv.at[me],
            send_sem=meta_ssem.at[d],
            recv_sem=meta_rsem.at[d],
            device_id={"sky": sky_at(d)},
            device_id_type=MESH,
        )

    def sky_copy(t, d):
        return pltpu.make_async_remote_copy(
            src_ref=x_send.at[t, sky_at(d)],
            dst_ref=x_recv.at[t, me],
            send_sem=x_ssem.at[t, d],
            recv_sem=x_rsem.at[t, d],
            device_id={"sky": sky_at(d)},
            device_id_type=MESH,
        )

    def band_copy(t, r, source, hop):
        return pltpu.make_async_remote_copy(
            src_ref=source.at[t],
            dst_ref=z_recv.at[hop, t],
            send_sem=z_ssem.at[t],
            recv_sem=z_rsem.at[hop, t],
            device_id={"band": band_at(r)},
            device_id_type=MESH,
        )

    def first_row(t):
        r, sub = chunk_of(t)
        return pl.multiple_of(band_at(r) * rows + sub * part, part)

    def convolve(t):
        rows_in = pl.ds(first_row(t), window)
        for s in range(pieces):
            first = jnp.dot(down[...], tiles[s, rows_in, :], preferred_element_type=F32)
            for k in range(basis):
                scale = jnp.broadcast_to(mixing[s, k : k + 1, :], (part, side))
                mixed[s * part : (s + 1) * part, k * side : (k + 1) * side] = (
                    first[k * part : (k + 1) * part] * scale
                ).astype(BF16)

        def second(_, carry):
            done = jnp.dot(mixed[...], across[...], preferred_element_type=F32)
            results[...] = done.astype(BF16).reshape(pieces, part, side)
            return carry

        once = lax.div(t, chunks) + 1
        lax.fori_loop(0, once, second, 0)

        def to_slots(_, carry):
            for slot in range(sky * cap):
                x_send[t, slot // cap, slot % cap] = results[slot_piece[slot]]
            for c in range(cap):
                x_recv[t, me, c] = results[slot_piece[me * cap + c]]
            return carry

        lax.fori_loop(0, once, to_slots, 0)

        @pl.when(t == 0)
        def _():
            pl.semaphore_wait(barrier, greeted)
            for d in range(1, sky):
                meta_copy(d).start()

        for d in range(1, sky):
            sky_copy(t, d).start()

    block = 16
    def collect(t):
        r, sub = chunk_of(t)

        @pl.when(t == 0)
        def _():
            for d in range(1, sky):
                meta_copy(d).wait()

        for d in range(1, sky):
            sky_copy(t, d).wait_recv()
        base = first_row(t)

        def some_rows(i, carry):
            spot = pl.ds(pl.multiple_of(i * block, block), block)
            line = lax.broadcasted_iota(jnp.int32, (block, 128), 0) + (base + i * block)
            line = line.astype(F32)
            lane = lax.broadcasted_iota(jnp.int32, (block, 128), 1).astype(F32)
            cover = jnp.zeros((block, 128), F32)
            sums = [jnp.zeros((block, side), F32) for _ in range(PATCH_DEV)]
            for src in range(sky):
                for c in range(cap):
                    weight = meta_recv[src, c : c + 1, :]
                    count = meta_recv[src, cap + c : cap + c + 1, :]
                    local = meta_recv[src, 2 * cap + c : 2 * cap + c + 1, :]
                    cover = cover + jnp.where((lane == local) & (line < count), weight, 0.0)
                    local = jnp.broadcast_to(local[:, :1], (block, side))
                    piece = x_recv[t, src, c, spot, :].astype(F32)
                    for p in range(PATCH_DEV):
                        sums[p] = sums[p] + jnp.where(local == float(p), piece, 0.0)
            scale = 1.0 / jnp.maximum(cover, 1.0)
            for p in range(PATCH_DEV):
                value = sums[p] * jnp.broadcast_to(scale[:, p : p + 1], (block, side))
                final[t, p, spot, :] = value.astype(BF16)
                coadd_ref[p, pl.ds(pl.multiple_of(base + i * block, block), block), :] = value
                values[lax.rem(t, 4), p, spot, :] = value
            return carry

        lax.fori_loop(0, part // block, some_rows, 0)

        @pl.when((r == 1) | ((r > 1) & (outer(r) == 1)))
        def _():
            band_copy(t, 1, final, 0).start()

        @pl.when(r == 0)
        def _():
            others = [(0, t - subs)] if bands > 1 else []
            for q in evens:
                through = up(q) * odd + (1 - up(q)) * (1 - odd)
                others.append((1, (bands - 2 - q) * subs + 2 * sub + 1 - through))
            for hop, other in others:
                band_copy(other, 1, final, hop).wait_recv()

            def add(p, carry):
                total = values[lax.rem(t, 4), p]
                for hop, other in others:
                    total = total + z_recv[hop, other, p].astype(F32)
                detect_ref[p, pl.ds(pl.multiple_of(sub * part, part), part), :] = total
                return carry

            lax.fori_loop(0, PATCH_DEV, add, 0)

    def forward(t, other):
        r = chunk_of(t)[0]

        @pl.when(outer(r) == 0)
        def _():
            band_copy(other, 1, final, 0).wait_recv()

            def add(p, carry):
                near = values[lax.rem(t, 4), p]
                stage[t, p] = (near + z_recv[0, other, p].astype(F32)).astype(BF16)
                return carry

            lax.fori_loop(0, PATCH_DEV, add, 0)
            band_copy(t, r, stage, 1).start()

    far = (bands - 2) * subs

    def forwards(t):
        if far <= 0:
            return

        @pl.when((lax.rem(t, 2) == 0) & (t >= 2) & (t <= far))
        def _():
            forward(t - 1, t - 2)

        @pl.when((lax.rem(t, 2) == 1) & (t >= 3) & (t <= far + 1))
        def _():
            forward(t - 3, t - 2)

    lag = 3

    def finish(t, carry):
        r = chunk_of(t)[0]
        for d in range(1, sky):
            sky_copy(t, d).wait_send()

        @pl.when(r > 0)
        def _():
            band_copy(t, 1, final, 0).wait_send()

        return carry

    held = 6

    def step(t, carry):
        @pl.when(t < chunks)
        def _():
            convolve(t)

        @pl.when(t >= lag)
        def _():
            collect(t - lag)
            forwards(t - lag)

        @pl.when(t >= lag + held)
        def _():
            finish(t - lag - held, 0)

        return carry

    lax.fori_loop(0, chunks + lag, step, 0)

    lax.fori_loop(max(0, chunks - held), chunks, finish, 0)


def put(coadd_in, detect_in, coadd_out, detect_out, sem):
    copies = [
        pltpu.make_async_copy(coadd_in.at[p], coadd_out.at[p], sem.at[p]) for p in range(PATCH_DEV)
    ]
    copies.append(pltpu.make_async_copy(detect_in, detect_out, sem.at[PATCH_DEV]))
    for copy in copies:
        copy.start()
    for copy in copies:
        copy.wait()


def per_device(
    patches, valid_rows, slot_owner, slot_local, slot_visit, basis_coef, inv_var, kernel_x, kernel_y
):
    pieces, side = patches.shape[1], patches.shape[2]
    basis, taps = kernel_x.shape
    sky, bands = lax.axis_size("sky"), lax.axis_size("band")
    cap = max(2, 2 * pieces // sky)
    rows = side // bands
    part = min(rows, 16)
    pad = -(-(taps // 2) // 16) * 16
    chunks = side // part
    meta_rows = -(-3 * cap // 8) * 8
    smem = pl.BlockSpec(memory_space=pltpu.SMEM)
    vmem = pl.BlockSpec(memory_space=pltpu.VMEM)
    hbm = pl.BlockSpec(memory_space=pl.ANY)
    sizes = (pieces, side, taps, basis, sky, bands, cap, rows, part, pad)
    coadd, detection = pl.pallas_call(
        functools.partial(kernel, sizes),
        out_shape=(
            pltpu.VMEM((PATCH_DEV, side, side), F32),
            pltpu.VMEM((PATCH_DEV, rows, side), F32),
        ),
        in_specs=[smem] * 5 + [hbm, vmem, vmem, vmem],
        out_specs=(vmem, vmem),
        scratch_shapes=[
            pltpu.VMEM((pieces, side, side), F32),
            pltpu.VMEM((pieces, side + 2 * pad, side), BF16),
            pltpu.VMEM((basis * part, part + 2 * pad), BF16),
            pltpu.VMEM((basis * side, side), BF16),
            pltpu.VMEM((pieces * part, basis * side), BF16),
            pltpu.VMEM((pieces, -(-basis // 8) * 8, side), F32),
            pltpu.VMEM((2 * basis, 128), F32),
            pltpu.VMEM((pieces, part, side), BF16),
            pltpu.SMEM((sky * cap,), jnp.int32),
            pltpu.VMEM((sky, meta_rows, 128), F32),
            pltpu.VMEM((sky, meta_rows, 128), F32),
            pltpu.VMEM((chunks, sky, cap, part, side), BF16),
            pltpu.VMEM((chunks, sky, cap, part, side), BF16),
            pltpu.VMEM((2, chunks, PATCH_DEV, part, side), BF16),
            pltpu.VMEM((chunks, PATCH_DEV, part, side), BF16),
            pltpu.VMEM((4, PATCH_DEV, part, side), F32),
            pltpu.VMEM((chunks, PATCH_DEV, part, side), BF16),
            pltpu.SemaphoreType.DMA((pieces,)),
            pltpu.SemaphoreType.DMA((sky,)),
            pltpu.SemaphoreType.DMA((sky,)),
            pltpu.SemaphoreType.DMA((chunks, sky)),
            pltpu.SemaphoreType.DMA((chunks, sky)),
            pltpu.SemaphoreType.DMA((chunks,)),
            pltpu.SemaphoreType.DMA((2, chunks)),
        ],
        compiler_params=pltpu.CompilerParams(
            collective_id=0, has_side_effects=True, vmem_limit_bytes=60 * 1024 * 1024
        ),
    )(
        valid_rows[0],
        slot_owner[0, :, 0],
        slot_local[0],
        slot_visit[0],
        inv_var[0],
        patches[0],
        jnp.transpose(basis_coef, (1, 0, 2)),
        kernel_x,
        kernel_y,
    )
    in_vmem = pltpu.MemorySpace.VMEM
    coadd, detection = pl.pallas_call(
        put,
        out_shape=(
            jax.ShapeDtypeStruct(coadd.shape, F32),
            jax.ShapeDtypeStruct(detection.shape, F32),
        ),
        in_specs=[vmem, vmem],
        out_specs=(hbm, hbm),
        scratch_shapes=[pltpu.SemaphoreType.DMA((PATCH_DEV + 1,))],
        compiler_params=pltpu.CompilerParams(vmem_limit_bytes=1024 * 1024),
    )(
        pltpu.with_memory_space_constraint(coadd, in_vmem),
        pltpu.with_memory_space_constraint(detection, in_vmem),
    )
    return coadd[None], detection


def solution(mesh):
    in_specs = (
        P(("tract", "band"), "sky", None, None),
        P(("tract", "band"), "sky"),
        P(("tract", "band"), "sky", None),
        P(("tract", "band"), "sky"),
        P(("tract", "band"), "sky"),
        P(("tract", "band"), None, None),
        P(("tract", "band"), None),
        P(),
        P(),
    )
    out_specs = (P(("tract", "band"), "sky", None, None), P(("tract", "sky"), "band", None))
    return jax.shard_map(
        per_device, mesh=mesh, in_specs=in_specs, out_specs=out_specs, check_vma=False
    )
```

```python
import functools

import jax
import jax.numpy as jnp
from jax import lax
from jax.experimental import pallas as pl
from jax.experimental.pallas import tpu as pltpu
from jax.sharding import PartitionSpec as P

PATCH_DEV = 8
MESH = pl.DeviceIdType.MESH
F32 = jnp.float32
BF16 = jnp.bfloat16


def chunk_at(t, bands, subs):
    if bands == 1:
        return t * 0, t
    far = (bands - 2) * subs
    near = lax.div(t, far) if far else t * 0 + 1
    pair = lax.rem(t, 2 * subs)
    last = t - far
    offset = (1 - near) * (bands - 1 - 2 * lax.div(t, 2 * subs) - lax.rem(pair, 2))
    offset = offset + near * (1 - lax.div(last, subs))
    return offset, (1 - near) * lax.div(pair, 2) + near * lax.rem(last, subs)


def flip(index, bits, top):
    result = index
    for i in range((top - 1).bit_length()):
        bit = lax.rem(lax.div(bits, 1 << i), 2)
        result = result + (1 << i) * bit * (1 - 2 * lax.rem(lax.div(index, 1 << i), 2))
    return result


def kernel(
    sizes,
    valid_ref,
    owner_ref,
    local_ref,
    visit_ref,
    ivar_ref,
    patches_ref,
    coef_ref,
    kx_ref,
    ky_ref,
    coadd_ref,
    detect_ref,
    raw,
    tiles,
    down,
    across,
    mixed,
    mixing,
    bases,
    results,
    slot_piece,
    meta_send,
    meta_recv,
    x_send,
    x_recv,
    z_recv,
    stage,
    values,
    final,
    load_sem,
    meta_ssem,
    meta_rsem,
    x_ssem,
    x_rsem,
    z_ssem,
    z_rsem,
):
    pieces, side, taps, basis, sky, bands, cap, rows, part, pad = sizes
    half = taps // 2
    window = part + 2 * pad
    me = lax.axis_index("sky")
    band = lax.axis_index("band")
    subs = rows // part
    chunks = bands * subs
    evens = list(range(2, bands, 2))

    def chunk_of(t):
        return chunk_at(jnp.int32(t), bands, subs)

    def band_at(r):
        return flip(band, jnp.int32(r), bands)

    def sky_at(d):
        return lax.rem(me + d, sky)

    loads = [
        pltpu.make_async_copy(patches_ref.at[s], raw.at[s], load_sem.at[s]) for s in range(pieces)
    ]
    for load in loads:
        load.start()

    barrier = pltpu.get_barrier_semaphore()
    for d in range(1, sky):
        pl.semaphore_signal(barrier, inc=1, device_id={"sky": sky_at(d)}, device_id_type=MESH)
    odd = lax.rem(band, 2)

    def up(r):
        return lax.div(band_at(r) - band - 1 + bands, bands)

    def outer(r):
        return up(r) * (1 - odd) + (1 - up(r)) * odd

    greeted = jnp.int32(sky - 1)
    for r in range(1, bands):

        def greet(r=r):
            pl.semaphore_signal(
                barrier, inc=1, device_id={"band": band_at(r)}, device_id_type=MESH
            )

        if r % 2 and r > 1:
            pl.when(outer(r) == 0)(greet)
            greeted = greeted + 1 - outer(r)
        else:
            greet()
            greeted = greeted + 1

    wide = bases.shape[1]
    taps_at = lax.broadcasted_iota(jnp.int32, (taps, wide), 0) - half
    lanes = lax.broadcasted_iota(jnp.int32, (taps, wide), 1)
    for start, ref, away in ((0, ky_ref, pad + taps_at), (basis, kx_ref, -taps_at)):
        place = (lanes == jnp.where(away < 0, away + wide, away)).astype(BF16)
        bases[start : start + basis, :] = jnp.dot(ref[...], place, preferred_element_type=F32)
    ring_row = lax.broadcasted_iota(jnp.int32, (wide, wide), 0)
    ring_col = lax.broadcasted_iota(jnp.int32, (wide, wide), 1)
    blocks = side // wide

    def make_tables(k, carry):
        row = jnp.broadcast_to(bases[pl.ds(k, 1), :], (part, wide))
        shifted = pltpu.roll(row, 0, 1, stride=1, stride_axis=0)
        down[pl.ds(pl.multiple_of(k * part, part), part), :] = shifted[:, :window].astype(BF16)
        row = jnp.broadcast_to(bases[pl.ds(basis + k, 1), :], (wide, wide))
        ring = pltpu.roll(row, 0, 1, stride=1, stride_axis=0)
        on = jnp.where(jnp.abs(ring_row - ring_col) <= half, ring, 0.0).astype(BF16)
        edge = -(-half // 16) * 16
        rest = jnp.zeros((wide - edge, wide), BF16)
        top = jnp.where(ring_col[:edge] - ring_row[:edge] >= wide - half, ring[:edge], 0.0)
        below = jnp.concatenate([top.astype(BF16), rest], axis=0)
        low = wide - edge
        end = jnp.where(ring_row[low:] - ring_col[low:] >= wide - half, ring[low:], 0.0)
        above = jnp.concatenate([rest, end.astype(BF16)], axis=0)
        none = jnp.zeros((wide, wide), BF16)
        pick = {0: on, 1: below, -1: above}
        for i in range(blocks):
            for j in range(blocks):
                spot = pl.ds(pl.multiple_of(k * side + i * wide, wide), wide)
                across[spot, j * wide : (j + 1) * wide] = pick.get(i - j, none)
        return carry

    lax.fori_loop(0, basis, make_tables, 0, unroll=7)

    owners = [owner_ref[s] for s in range(pieces)]
    ranks = []
    for s in range(pieces):
        rank = jnp.int32(0)
        for other in range(s):
            rank = rank + (owners[other] == owners[s]).astype(jnp.int32)
        ranks.append(owners[s] * cap + rank)
    tall = -(-basis // 8) * 8
    on_lane = lax.broadcasted_iota(jnp.int32, (tall, basis), 1)
    on_row = lax.broadcasted_iota(jnp.int32, (tall, basis), 0)
    for s in range(pieces):
        weight = jnp.full((1, basis), ivar_ref[visit_ref[s]], F32).astype(BF16).astype(F32)
        coefs = coef_ref[visit_ref[s]].astype(BF16).astype(F32)
        mix = (coefs * weight).astype(BF16).astype(F32)
        column = jnp.sum(
            jnp.where(on_lane == on_row, jnp.broadcast_to(mix, (tall, basis)), 0.0),
            axis=1,
            keepdims=True,
        )
        mixing[s] = jnp.broadcast_to(column, (tall, side))
    for slot in range(sky * cap):
        piece = jnp.int32(0)
        used = jnp.int32(0)
        for s in range(pieces):
            hit = (ranks[s] == slot).astype(jnp.int32)
            piece = piece + hit * s
            used = used + hit
        slot_piece[slot] = piece
        dest, c = divmod(slot, cap)
        meta_send[dest, c : c + 1, :] = (
            jnp.full((1, 128), ivar_ref[visit_ref[piece]], F32).astype(BF16).astype(F32)
        )
        meta_send[dest, cap + c : cap + c + 1, :] = jnp.full(
            (1, 128), valid_ref[piece], jnp.int32
        ).astype(F32)
        meta_send[dest, 2 * cap + c : 2 * cap + c + 1, :] = jnp.full(
            (1, 128), local_ref[piece] * used + used - 1, jnp.int32
        ).astype(F32)
    meta_recv[me] = meta_send[me]

    row_ids = lax.broadcasted_iota(jnp.int32, (side, side), 0)
    for s in range(pieces):
        tiles[s, 0:pad, :] = jnp.zeros((pad, side), BF16)
        tiles[s, pad + side : side + 2 * pad, :] = jnp.zeros((pad, side), BF16)
        loads[s].wait()
        tiles[s, pad : pad + side, :] = jnp.where(row_ids < valid_ref[s], raw[s], 0.0).astype(BF16)

    def meta_copy(d):
        return pltpu.make_async_remote_copy(
            src_ref=meta_send.at[sky_at(d)],
            dst_ref=meta_recv.at[me],
            send_sem=meta_ssem.at[d],
            recv_sem=meta_rsem.at[d],
            device_id={"sky": sky_at(d)},
            device_id_type=MESH,
        )

    def sky_copy(t, d):
        return pltpu.make_async_remote_copy(
            src_ref=x_send.at[t, sky_at(d)],
            dst_ref=x_recv.at[t, me],
            send_sem=x_ssem.at[t, d],
            recv_sem=x_rsem.at[t, d],
            device_id={"sky": sky_at(d)},
            device_id_type=MESH,
        )

    def band_copy(t, r, source, hop):
        return pltpu.make_async_remote_copy(
            src_ref=source.at[t],
            dst_ref=z_recv.at[hop, t],
            send_sem=z_ssem.at[t],
            recv_sem=z_rsem.at[hop, t],
            device_id={"band": band_at(r)},
            device_id_type=MESH,
        )

    def first_row(t):
        r, sub = chunk_of(t)
        return pl.multiple_of(band_at(r) * rows + sub * part, part)

    def convolve(t):
        rows_in = pl.ds(first_row(t), window)
        for s in range(pieces):
            first = jnp.dot(down[...], tiles[s, rows_in, :], preferred_element_type=F32)
            for k in range(basis):
                scale = jnp.broadcast_to(mixing[s, k : k + 1, :], (part, side))
                mixed[s * part : (s + 1) * part, k * side : (k + 1) * side] = (
                    first[k * part : (k + 1) * part] * scale
                ).astype(BF16)

        def second(_, carry):
            done = jnp.dot(mixed[...], across[...], preferred_element_type=F32)
            results[...] = done.astype(BF16).reshape(pieces, part, side)
            return carry

        once = lax.div(t, chunks) + 1
        lax.fori_loop(0, once, second, 0)

        def to_slots(_, carry):
            for slot in range(sky * cap):
                x_send[t, slot // cap, slot % cap] = results[slot_piece[slot]]
            for c in range(cap):
                x_recv[t, me, c] = results[slot_piece[me * cap + c]]
            return carry

        lax.fori_loop(0, once, to_slots, 0)

        @pl.when(t == 0)
        def _():
            pl.semaphore_wait(barrier, greeted)
            for d in range(1, sky):
                meta_copy(d).start()

        for d in range(1, sky):
            sky_copy(t, d).start()

    block = 16
    def collect(t):
        r, sub = chunk_of(t)

        @pl.when(t == 0)
        def _():
            for d in range(1, sky):
                meta_copy(d).wait()

        for d in range(1, sky):
            sky_copy(t, d).wait_recv()
        base = first_row(t)

        def some_rows(i, carry):
            spot = pl.ds(pl.multiple_of(i * block, block), block)
            line = lax.broadcasted_iota(jnp.int32, (block, 128), 0) + (base + i * block)
            line = line.astype(F32)
            lane = lax.broadcasted_iota(jnp.int32, (block, 128), 1).astype(F32)
            cover = jnp.zeros((block, 128), F32)
            sums = [jnp.zeros((block, side), F32) for _ in range(PATCH_DEV)]
            for src in range(sky):
                for c in range(cap):
                    weight = meta_recv[src, c : c + 1, :]
                    count = meta_recv[src, cap + c : cap + c + 1, :]
                    local = meta_recv[src, 2 * cap + c : 2 * cap + c + 1, :]
                    cover = cover + jnp.where((lane == local) & (line < count), weight, 0.0)
                    local = jnp.broadcast_to(local[:, :1], (block, side))
                    piece = x_recv[t, src, c, spot, :].astype(F32)
                    for p in range(PATCH_DEV):
                        sums[p] = sums[p] + jnp.where(local == float(p), piece, 0.0)
            scale = 1.0 / jnp.maximum(cover, 1.0)
            for p in range(PATCH_DEV):
                value = sums[p] * jnp.broadcast_to(scale[:, p : p + 1], (block, side))
                final[t, p, spot, :] = value.astype(BF16)
                coadd_ref[p, pl.ds(pl.multiple_of(base + i * block, block), block), :] = value
                values[lax.rem(t, 4), p, spot, :] = value
            return carry

        lax.fori_loop(0, part // block, some_rows, 0)

        @pl.when((r == 1) | ((r > 1) & (outer(r) == 1)))
        def _():
            band_copy(t, 1, final, 0).start()

        @pl.when(r == 0)
        def _():
            others = [(0, t - subs)] if bands > 1 else []
            for q in evens:
                through = up(q) * odd + (1 - up(q)) * (1 - odd)
                others.append((1, (bands - 2 - q) * subs + 2 * sub + 1 - through))
            for hop, other in others:
                band_copy(other, 1, final, hop).wait_recv()

            def add(p, carry):
                total = values[lax.rem(t, 4), p]
                for hop, other in others:
                    total = total + z_recv[hop, other, p].astype(F32)
                detect_ref[p, pl.ds(pl.multiple_of(sub * part, part), part), :] = total
                return carry

            lax.fori_loop(0, PATCH_DEV, add, 0)

    def forward(t, other):
        r = chunk_of(t)[0]

        @pl.when(outer(r) == 0)
        def _():
            band_copy(other, 1, final, 0).wait_recv()

            def add(p, carry):
                near = values[lax.rem(t, 4), p]
                stage[t, p] = (near + z_recv[0, other, p].astype(F32)).astype(BF16)
                return carry

            lax.fori_loop(0, PATCH_DEV, add, 0)
            band_copy(t, r, stage, 1).start()

    far = (bands - 2) * subs

    def forwards(t):
        if far <= 0:
            return

        @pl.when((lax.rem(t, 2) == 0) & (t >= 2) & (t <= far))
        def _():
            forward(t - 1, t - 2)

        @pl.when((lax.rem(t, 2) == 1) & (t >= 3) & (t <= far + 1))
        def _():
            forward(t - 3, t - 2)

    lag = 3

    def finish(t, carry):
        r = chunk_of(t)[0]
        for d in range(1, sky):
            sky_copy(t, d).wait_send()

        @pl.when(r > 0)
        def _():
            band_copy(t, 1, final, 0).wait_send()

        return carry

    held = 6

    def step(t, carry):
        @pl.when(t < chunks)
        def _():
            convolve(t)

        @pl.when(t >= lag)
        def _():
            collect(t - lag)
            forwards(t - lag)

        @pl.when(t >= lag + held)
        def _():
            finish(t - lag - held, 0)

        return carry

    lax.fori_loop(0, chunks + lag, step, 0)

    lax.fori_loop(max(0, chunks - held), chunks, finish, 0)


def put(coadd_in, detect_in, coadd_out, detect_out, sem):
    copies = [
        pltpu.make_async_copy(coadd_in.at[p], coadd_out.at[p], sem.at[p]) for p in range(PATCH_DEV)
    ]
    copies.append(pltpu.make_async_copy(detect_in, detect_out, sem.at[PATCH_DEV]))
    for copy in copies:
        copy.start()
    for copy in copies:
        copy.wait()


def per_device(
    patches, valid_rows, slot_owner, slot_local, slot_visit, basis_coef, inv_var, kernel_x, kernel_y
):
    pieces, side = patches.shape[1], patches.shape[2]
    basis, taps = kernel_x.shape
    sky, bands = lax.axis_size("sky"), lax.axis_size("band")
    cap = max(2, 2 * pieces // sky)
    rows = side // bands
    part = min(rows, 16)
    pad = -(-(taps // 2) // 16) * 16
    chunks = side // part
    meta_rows = -(-3 * cap // 8) * 8
    smem = pl.BlockSpec(memory_space=pltpu.SMEM)
    vmem = pl.BlockSpec(memory_space=pltpu.VMEM)
    hbm = pl.BlockSpec(memory_space=pl.ANY)
    sizes = (pieces, side, taps, basis, sky, bands, cap, rows, part, pad)
    coadd, detection = pl.pallas_call(
        functools.partial(kernel, sizes),
        out_shape=(
            pltpu.VMEM((PATCH_DEV, side, side), F32),
            pltpu.VMEM((PATCH_DEV, rows, side), F32),
        ),
        in_specs=[smem] * 5 + [hbm, vmem, vmem, vmem],
        out_specs=(vmem, vmem),
        scratch_shapes=[
            pltpu.VMEM((pieces, side, side), F32),
            pltpu.VMEM((pieces, side + 2 * pad, side), BF16),
            pltpu.VMEM((basis * part, part + 2 * pad), BF16),
            pltpu.VMEM((basis * side, side), BF16),
            pltpu.VMEM((pieces * part, basis * side), BF16),
            pltpu.VMEM((pieces, -(-basis // 8) * 8, side), F32),
            pltpu.VMEM((2 * basis, 128), F32),
            pltpu.VMEM((pieces, part, side), BF16),
            pltpu.SMEM((sky * cap,), jnp.int32),
            pltpu.VMEM((sky, meta_rows, 128), F32),
            pltpu.VMEM((sky, meta_rows, 128), F32),
            pltpu.VMEM((chunks, sky, cap, part, side), BF16),
            pltpu.VMEM((chunks, sky, cap, part, side), BF16),
            pltpu.VMEM((2, chunks, PATCH_DEV, part, side), BF16),
            pltpu.VMEM((chunks, PATCH_DEV, part, side), BF16),
            pltpu.VMEM((4, PATCH_DEV, part, side), F32),
            pltpu.VMEM((chunks, PATCH_DEV, part, side), BF16),
            pltpu.SemaphoreType.DMA((pieces,)),
            pltpu.SemaphoreType.DMA((sky,)),
            pltpu.SemaphoreType.DMA((sky,)),
            pltpu.SemaphoreType.DMA((chunks, sky)),
            pltpu.SemaphoreType.DMA((chunks, sky)),
            pltpu.SemaphoreType.DMA((chunks,)),
            pltpu.SemaphoreType.DMA((2, chunks)),
        ],
        compiler_params=pltpu.CompilerParams(
            collective_id=0, has_side_effects=True, vmem_limit_bytes=60 * 1024 * 1024
        ),
    )(
        valid_rows[0],
        slot_owner[0, :, 0],
        slot_local[0],
        slot_visit[0],
        inv_var[0],
        patches[0],
        jnp.transpose(basis_coef, (1, 0, 2)),
        kernel_x,
        kernel_y,
    )
    in_vmem = pltpu.MemorySpace.VMEM
    coadd, detection = pl.pallas_call(
        put,
        out_shape=(
            jax.ShapeDtypeStruct(coadd.shape, F32),
            jax.ShapeDtypeStruct(detection.shape, F32),
        ),
        in_specs=[vmem, vmem],
        out_specs=(hbm, hbm),
        scratch_shapes=[pltpu.SemaphoreType.DMA((PATCH_DEV + 1,))],
        compiler_params=pltpu.CompilerParams(vmem_limit_bytes=1024 * 1024),
    )(
        pltpu.with_memory_space_constraint(coadd, in_vmem),
        pltpu.with_memory_space_constraint(detection, in_vmem),
    )
    return coadd[None], detection


def solution(mesh):
    in_specs = (
        P(("tract", "band"), "sky", None, None),
        P(("tract", "band"), "sky"),
        P(("tract", "band"), "sky", None),
        P(("tract", "band"), "sky"),
        P(("tract", "band"), "sky"),
        P(("tract", "band"), None, None),
        P(("tract", "band"), None),
        P(),
        P(),
    )
    out_specs = (P(("tract", "band"), "sky", None, None), P(("tract", "sky"), "band", None))
    return jax.shard_map(
        per_device, mesh=mesh, in_specs=in_specs, out_specs=out_specs, check_vma=False
    )
```

```python
import functools

import jax
import jax.numpy as jnp
from jax import lax
from jax.experimental import pallas as pl
from jax.experimental.pallas import tpu as pltpu
from jax.sharding import PartitionSpec as P

PATCH_DEV = 8
MESH = pl.DeviceIdType.MESH
F32 = jnp.float32
BF16 = jnp.bfloat16


def chunk_at(t, bands, subs):
    if bands == 1:
        return t * 0, t
    far = (bands - 2) * subs
    near = lax.div(t, far) if far else t * 0 + 1
    pair = lax.rem(t, 2 * subs)
    last = t - far
    offset = (1 - near) * (bands - 1 - 2 * lax.div(t, 2 * subs) - lax.rem(pair, 2))
    offset = offset + near * (1 - lax.div(last, subs))
    return offset, (1 - near) * lax.div(pair, 2) + near * lax.rem(last, subs)


def flip(index, bits, top):
    result = index
    for i in range((top - 1).bit_length()):
        bit = lax.rem(lax.div(bits, 1 << i), 2)
        result = result + (1 << i) * bit * (1 - 2 * lax.rem(lax.div(index, 1 << i), 2))
    return result


def kernel(
    sizes,
    valid_ref,
    owner_ref,
    local_ref,
    visit_ref,
    ivar_ref,
    patches_ref,
    coef_ref,
    kx_ref,
    ky_ref,
    coadd_ref,
    detect_ref,
    raw,
    tiles,
    down,
    across,
    mixed,
    mixing,
    bases,
    results,
    slot_piece,
    meta_send,
    meta_recv,
    x_send,
    x_recv,
    z_recv,
    stage,
    values,
    final,
    load_sem,
    meta_ssem,
    meta_rsem,
    x_ssem,
    x_rsem,
    z_ssem,
    z_rsem,
):
    pieces, side, taps, basis, sky, bands, cap, rows, part, pad = sizes
    half = taps // 2
    window = part + 2 * pad
    me = lax.axis_index("sky")
    band = lax.axis_index("band")
    subs = rows // part
    chunks = bands * subs
    evens = list(range(2, bands, 2))

    def chunk_of(t):
        return chunk_at(jnp.int32(t), bands, subs)

    def band_at(r):
        return flip(band, jnp.int32(r), bands)

    def sky_at(d):
        return lax.rem(me + d, sky)

    loads = [
        pltpu.make_async_copy(
            patches_ref.at[s, pl.ds(i * side // 2, side // 2)],
            raw.at[s, pl.ds(i * side // 2, side // 2)],
            load_sem.at[2 * s + i],
        )
        for s in range(pieces)
        for i in range(2)
    ]
    for load in loads:
        load.start()

    barrier = pltpu.get_barrier_semaphore()
    for d in range(1, sky):
        pl.semaphore_signal(barrier, inc=1, device_id={"sky": sky_at(d)}, device_id_type=MESH)
    odd = lax.rem(band, 2)

    def up(r):
        return lax.div(band_at(r) - band - 1 + bands, bands)

    def outer(r):
        return up(r) * (1 - odd) + (1 - up(r)) * odd

    greeted = jnp.int32(sky - 1)
    for r in range(1, bands):

        def greet(r=r):
            pl.semaphore_signal(
                barrier, inc=1, device_id={"band": band_at(r)}, device_id_type=MESH
            )

        if r % 2 and r > 1:
            pl.when(outer(r) == 0)(greet)
            greeted = greeted + 1 - outer(r)
        else:
            greet()
            greeted = greeted + 1

    wide = bases.shape[1]
    taps_at = lax.broadcasted_iota(jnp.int32, (taps, wide), 0) - half
    lanes = lax.broadcasted_iota(jnp.int32, (taps, wide), 1)
    for start, ref, away in ((0, ky_ref, pad + taps_at), (basis, kx_ref, -taps_at)):
        place = (lanes == jnp.where(away < 0, away + wide, away)).astype(BF16)
        bases[start : start + basis, :] = jnp.dot(ref[...], place, preferred_element_type=F32)
    ring_row = lax.broadcasted_iota(jnp.int32, (wide, wide), 0)
    ring_col = lax.broadcasted_iota(jnp.int32, (wide, wide), 1)
    blocks = side // wide

    def make_tables(k, carry):
        row = jnp.broadcast_to(bases[pl.ds(k, 1), :], (part, wide))
        shifted = pltpu.roll(row, 0, 1, stride=1, stride_axis=0)
        down[pl.ds(pl.multiple_of(k * part, part), part), :] = shifted[:, :window].astype(BF16)
        row = jnp.broadcast_to(bases[pl.ds(basis + k, 1), :], (wide, wide))
        ring = pltpu.roll(row, 0, 1, stride=1, stride_axis=0)
        on = jnp.where(jnp.abs(ring_row - ring_col) <= half, ring, 0.0).astype(BF16)
        edge = -(-half // 16) * 16
        rest = jnp.zeros((wide - edge, wide), BF16)
        top = jnp.where(ring_col[:edge] - ring_row[:edge] >= wide - half, ring[:edge], 0.0)
        below = jnp.concatenate([top.astype(BF16), rest], axis=0)
        low = wide - edge
        end = jnp.where(ring_row[low:] - ring_col[low:] >= wide - half, ring[low:], 0.0)
        above = jnp.concatenate([rest, end.astype(BF16)], axis=0)
        none = jnp.zeros((wide, wide), BF16)
        pick = {0: on, 1: below, -1: above}
        for i in range(blocks):
            for j in range(blocks):
                spot = pl.ds(pl.multiple_of(k * side + i * wide, wide), wide)
                across[spot, j * wide : (j + 1) * wide] = pick.get(i - j, none)
        return carry

    lax.fori_loop(0, basis, make_tables, 0, unroll=3)

    owners = [owner_ref[s] for s in range(pieces)]
    ranks = []
    for s in range(pieces):
        rank = jnp.int32(0)
        for other in range(s):
            rank = rank + (owners[other] == owners[s]).astype(jnp.int32)
        ranks.append(owners[s] * cap + rank)
    tall = -(-basis // 8) * 8
    on_lane = lax.broadcasted_iota(jnp.int32, (tall, basis), 1)
    on_row = lax.broadcasted_iota(jnp.int32, (tall, basis), 0)
    for s in range(pieces):
        weight = jnp.full((1, basis), ivar_ref[visit_ref[s]], F32).astype(BF16).astype(F32)
        coefs = coef_ref[visit_ref[s]].astype(BF16).astype(F32)
        mix = (coefs * weight).astype(BF16).astype(F32)
        column = jnp.sum(
            jnp.where(on_lane == on_row, jnp.broadcast_to(mix, (tall, basis)), 0.0),
            axis=1,
            keepdims=True,
        )
        mixing[s] = jnp.broadcast_to(column, (tall, side))
    for slot in range(sky * cap):
        piece = jnp.int32(0)
        used = jnp.int32(0)
        for s in range(pieces):
            hit = (ranks[s] == slot).astype(jnp.int32)
            piece = piece + hit * s
            used = used + hit
        slot_piece[slot] = piece
        dest, c = divmod(slot, cap)
        meta_send[dest, c : c + 1, :] = (
            jnp.full((1, 128), ivar_ref[visit_ref[piece]], F32).astype(BF16).astype(F32)
        )
        meta_send[dest, cap + c : cap + c + 1, :] = jnp.full(
            (1, 128), valid_ref[piece], jnp.int32
        ).astype(F32)
        meta_send[dest, 2 * cap + c : 2 * cap + c + 1, :] = jnp.full(
            (1, 128), local_ref[piece] * used + used - 1, jnp.int32
        ).astype(F32)
    meta_recv[me] = meta_send[me]

    row_ids = lax.broadcasted_iota(jnp.int32, (side, side), 0)
    for s in range(pieces):
        tiles[s, 0:pad, :] = jnp.zeros((pad, side), BF16)
        tiles[s, pad + side : side + 2 * pad, :] = jnp.zeros((pad, side), BF16)
        loads[2 * s].wait()
        loads[2 * s + 1].wait()
        tiles[s, pad : pad + side, :] = jnp.where(row_ids < valid_ref[s], raw[s], 0.0).astype(BF16)

    def meta_copy(d):
        return pltpu.make_async_remote_copy(
            src_ref=meta_send.at[sky_at(d)],
            dst_ref=meta_recv.at[me],
            send_sem=meta_ssem.at[d],
            recv_sem=meta_rsem.at[d],
            device_id={"sky": sky_at(d)},
            device_id_type=MESH,
        )

    def sky_copy(t, d):
        return pltpu.make_async_remote_copy(
            src_ref=x_send.at[t, sky_at(d)],
            dst_ref=x_recv.at[t, me],
            send_sem=x_ssem.at[t, d],
            recv_sem=x_rsem.at[t, d],
            device_id={"sky": sky_at(d)},
            device_id_type=MESH,
        )

    def band_copy(t, r, source, hop):
        return pltpu.make_async_remote_copy(
            src_ref=source.at[t],
            dst_ref=z_recv.at[hop, t],
            send_sem=z_ssem.at[t],
            recv_sem=z_rsem.at[hop, t],
            device_id={"band": band_at(r)},
            device_id_type=MESH,
        )

    def first_row(t):
        r, sub = chunk_of(t)
        return pl.multiple_of(band_at(r) * rows + sub * part, part)

    def convolve(t):
        rows_in = pl.ds(first_row(t), window)
        for s in range(pieces):
            first = jnp.dot(down[...], tiles[s, rows_in, :], preferred_element_type=F32)
            for k in range(basis):
                scale = jnp.broadcast_to(mixing[s, k : k + 1, :], (part, side))
                mixed[s * part : (s + 1) * part, k * side : (k + 1) * side] = (
                    first[k * part : (k + 1) * part] * scale
                ).astype(BF16)

        def second(_, carry):
            done = jnp.dot(mixed[...], across[...], preferred_element_type=F32)
            results[...] = done.astype(BF16).reshape(pieces, part, side)
            return carry

        once = lax.div(t, chunks) + 1
        lax.fori_loop(0, once, second, 0)

        def to_slots(_, carry):
            for slot in range(sky * cap):
                x_send[t, slot // cap, slot % cap] = results[slot_piece[slot]]
            for c in range(cap):
                x_recv[t, me, c] = results[slot_piece[me * cap + c]]
            return carry

        lax.fori_loop(0, once, to_slots, 0)

        @pl.when(t == 0)
        def _():
            pl.semaphore_wait(barrier, greeted)
            for d in range(1, sky):
                meta_copy(d).start()

        for d in range(1, sky):
            sky_copy(t, d).start()

    block = 16
    def collect(t):
        r, sub = chunk_of(t)

        @pl.when(t == 0)
        def _():
            for d in range(1, sky):
                meta_copy(d).wait()

        for d in range(1, sky):
            sky_copy(t, d).wait_recv()
        base = first_row(t)

        def some_rows(i, carry):
            spot = pl.ds(pl.multiple_of(i * block, block), block)
            line = lax.broadcasted_iota(jnp.int32, (block, 128), 0) + (base + i * block)
            line = line.astype(F32)
            lane = lax.broadcasted_iota(jnp.int32, (block, 128), 1).astype(F32)
            cover = jnp.zeros((block, 128), F32)
            sums = [jnp.zeros((block, side), F32) for _ in range(PATCH_DEV)]
            for src in range(sky):
                for c in range(cap):
                    weight = meta_recv[src, c : c + 1, :]
                    count = meta_recv[src, cap + c : cap + c + 1, :]
                    local = meta_recv[src, 2 * cap + c : 2 * cap + c + 1, :]
                    cover = cover + jnp.where((lane == local) & (line < count), weight, 0.0)
                    local = jnp.broadcast_to(local[:, :1], (block, side))
                    piece = x_recv[t, src, c, spot, :].astype(F32)
                    for p in range(PATCH_DEV):
                        sums[p] = sums[p] + jnp.where(local == float(p), piece, 0.0)
            scale = 1.0 / jnp.maximum(cover, 1.0)
            for p in range(PATCH_DEV):
                value = sums[p] * jnp.broadcast_to(scale[:, p : p + 1], (block, side))
                final[t, p, spot, :] = value.astype(BF16)
                coadd_ref[p, pl.ds(pl.multiple_of(base + i * block, block), block), :] = value
                values[lax.rem(t, 4), p, spot, :] = value
            return carry

        lax.fori_loop(0, part // block, some_rows, 0)

        @pl.when((r == 1) | ((r > 1) & (outer(r) == 1)))
        def _():
            band_copy(t, 1, final, 0).start()

        @pl.when(r == 0)
        def _():
            others = [(0, t - subs)] if bands > 1 else []
            for q in evens:
                through = up(q) * odd + (1 - up(q)) * (1 - odd)
                others.append((1, (bands - 2 - q) * subs + 2 * sub + 1 - through))
            for hop, other in others:
                band_copy(other, 1, final, hop).wait_recv()

            def add(p, carry):
                total = values[lax.rem(t, 4), p]
                for hop, other in others:
                    total = total + z_recv[hop, other, p].astype(F32)
                detect_ref[p, pl.ds(pl.multiple_of(sub * part, part), part), :] = total
                return carry

            lax.fori_loop(0, PATCH_DEV, add, 0)

    def forward(t, other):
        r = chunk_of(t)[0]

        @pl.when(outer(r) == 0)
        def _():
            band_copy(other, 1, final, 0).wait_recv()

            def add(p, carry):
                near = values[lax.rem(t, 4), p]
                stage[t, p] = (near + z_recv[0, other, p].astype(F32)).astype(BF16)
                return carry

            lax.fori_loop(0, PATCH_DEV, add, 0)
            band_copy(t, r, stage, 1).start()

    far = (bands - 2) * subs

    def forwards(t):
        if far <= 0:
            return

        @pl.when((lax.rem(t, 2) == 0) & (t >= 2) & (t <= far))
        def _():
            forward(t - 1, t - 2)

        @pl.when((lax.rem(t, 2) == 1) & (t >= 3) & (t <= far + 1))
        def _():
            forward(t - 3, t - 2)

    lag = 3

    def finish(t, carry):
        r = chunk_of(t)[0]
        for d in range(1, sky):
            sky_copy(t, d).wait_send()

        @pl.when(r > 0)
        def _():
            band_copy(t, 1, final, 0).wait_send()

        return carry

    held = 6

    def step(t, carry):
        @pl.when(t < chunks)
        def _():
            convolve(t)

        @pl.when(t >= lag)
        def _():
            collect(t - lag)
            forwards(t - lag)

        @pl.when(t >= lag + held)
        def _():
            finish(t - lag - held, 0)

        return carry

    lax.fori_loop(0, chunks + lag, step, 0)

    lax.fori_loop(max(0, chunks - held), chunks, finish, 0)


def put(coadd_in, detect_in, coadd_out, detect_out, sem):
    copies = [
        pltpu.make_async_copy(coadd_in.at[p], coadd_out.at[p], sem.at[p]) for p in range(PATCH_DEV)
    ]
    copies.append(pltpu.make_async_copy(detect_in, detect_out, sem.at[PATCH_DEV]))
    for copy in copies:
        copy.start()
    for copy in copies:
        copy.wait()


def per_device(
    patches, valid_rows, slot_owner, slot_local, slot_visit, basis_coef, inv_var, kernel_x, kernel_y
):
    pieces, side = patches.shape[1], patches.shape[2]
    basis, taps = kernel_x.shape
    sky, bands = lax.axis_size("sky"), lax.axis_size("band")
    cap = max(2, 2 * pieces // sky)
    rows = side // bands
    part = min(rows, 16)
    pad = -(-(taps // 2) // 16) * 16
    chunks = side // part
    meta_rows = -(-3 * cap // 8) * 8
    smem = pl.BlockSpec(memory_space=pltpu.SMEM)
    vmem = pl.BlockSpec(memory_space=pltpu.VMEM)
    hbm = pl.BlockSpec(memory_space=pl.ANY)
    sizes = (pieces, side, taps, basis, sky, bands, cap, rows, part, pad)
    coadd, detection = pl.pallas_call(
        functools.partial(kernel, sizes),
        out_shape=(
            pltpu.VMEM((PATCH_DEV, side, side), F32),
            pltpu.VMEM((PATCH_DEV, rows, side), F32),
        ),
        in_specs=[smem] * 5 + [hbm, vmem, vmem, vmem],
        out_specs=(vmem, vmem),
        scratch_shapes=[
            pltpu.VMEM((pieces, side, side), F32),
            pltpu.VMEM((pieces, side + 2 * pad, side), BF16),
            pltpu.VMEM((basis * part, part + 2 * pad), BF16),
            pltpu.VMEM((basis * side, side), BF16),
            pltpu.VMEM((pieces * part, basis * side), BF16),
            pltpu.VMEM((pieces, -(-basis // 8) * 8, side), F32),
            pltpu.VMEM((2 * basis, 128), F32),
            pltpu.VMEM((pieces, part, side), BF16),
            pltpu.SMEM((sky * cap,), jnp.int32),
            pltpu.VMEM((sky, meta_rows, 128), F32),
            pltpu.VMEM((sky, meta_rows, 128), F32),
            pltpu.VMEM((chunks, sky, cap, part, side), BF16),
            pltpu.VMEM((chunks, sky, cap, part, side), BF16),
            pltpu.VMEM((2, chunks, PATCH_DEV, part, side), BF16),
            pltpu.VMEM((chunks, PATCH_DEV, part, side), BF16),
            pltpu.VMEM((4, PATCH_DEV, part, side), F32),
            pltpu.VMEM((chunks, PATCH_DEV, part, side), BF16),
            pltpu.SemaphoreType.DMA((2 * pieces,)),
            pltpu.SemaphoreType.DMA((sky,)),
            pltpu.SemaphoreType.DMA((sky,)),
            pltpu.SemaphoreType.DMA((chunks, sky)),
            pltpu.SemaphoreType.DMA((chunks, sky)),
            pltpu.SemaphoreType.DMA((chunks,)),
            pltpu.SemaphoreType.DMA((2, chunks)),
        ],
        compiler_params=pltpu.CompilerParams(
            collective_id=0, has_side_effects=True, vmem_limit_bytes=60 * 1024 * 1024
        ),
    )(
        valid_rows[0],
        slot_owner[0, :, 0],
        slot_local[0],
        slot_visit[0],
        inv_var[0],
        patches[0],
        jnp.transpose(basis_coef, (1, 0, 2)),
        kernel_x,
        kernel_y,
    )
    in_vmem = pltpu.MemorySpace.VMEM
    coadd, detection = pl.pallas_call(
        put,
        out_shape=(
            jax.ShapeDtypeStruct(coadd.shape, F32),
            jax.ShapeDtypeStruct(detection.shape, F32),
        ),
        in_specs=[vmem, vmem],
        out_specs=(hbm, hbm),
        scratch_shapes=[pltpu.SemaphoreType.DMA((PATCH_DEV + 1,))],
        compiler_params=pltpu.CompilerParams(vmem_limit_bytes=1024 * 1024),
    )(
        pltpu.with_memory_space_constraint(coadd, in_vmem),
        pltpu.with_memory_space_constraint(detection, in_vmem),
    )
    return coadd[None], detection


def solution(mesh):
    in_specs = (
        P(("tract", "band"), "sky", None, None),
        P(("tract", "band"), "sky"),
        P(("tract", "band"), "sky", None),
        P(("tract", "band"), "sky"),
        P(("tract", "band"), "sky"),
        P(("tract", "band"), None, None),
        P(("tract", "band"), None),
        P(),
        P(),
    )
    out_specs = (P(("tract", "band"), "sky", None, None), P(("tract", "sky"), "band", None))
    return jax.shard_map(
        per_device, mesh=mesh, in_specs=in_specs, out_specs=out_specs, check_vma=False
    )
```
